256 devices in a mesh: filt: 16 (over y, z_hi), chan: 4 (over x), tile: 4 (over z_lo, core).
Axes of the slice: x: 4, y: 4, z: 8 (z_hi: 4, z_lo: 2; z = z_hi * 2 + z_lo), core: 2. Of those that a mesh axis runs over, the one named last changes fastest.
Arguments:
- saved_input: bfloat16 [256, 48, 2048], P('tile', 'filt', 'chan'), may hold values from -1.5 to 1.5
- upstream: bfloat16 [256, 48, 2048], P('tile', None, 'filt'), may hold values from -4 to 4
- kernel: bfloat16 [3, 3, 2048, 2048], P(None, None, 'chan', 'filt'), may hold values from -0.046875 to 0.046875
Outputs:
- input_grad: bfloat16 [256, 48, 2048], P('tile', 'filt', 'chan')
- kernel_grad: float32 [3, 3, 2048, 2048], P(None, None, ('chan', 'tile'), 'filt')
The draws below stay inside these ranges and needn't reach their ends.
All inputs are finite; a program needn't handle non-finite values.
Results may differ from the reference program's by a relative error of at most 0.014.
Values may be sent and summed in bfloat16 or wider, within the bound.
A program may use at most 128 MiB of HBM per device.

```python
import jax
import jax.numpy as jnp
from jax import lax

CIN = 2048
COUT = 2048
TILE_COLS = 48
HEIGHT = 256
N_FILT = 16


def block_scale(key, shape, cuts, least, high):
    loudness, own = 1.0, jax.random.fold_in(key, 6)
    for dim, parts in cuts:
        draws = jnp.exp(jax.random.uniform(jax.random.fold_in(own, dim), (parts,), jnp.float32, least / len(cuts), high / len(cuts)))
        loudness = loudness * jnp.repeat(draws, shape[dim] // parts).reshape([-1 if axis == dim else 1 for axis in range(len(shape))])
    return loudness


def centred(stream_key, extent, deviation, most, cuts=(), kind=jnp.bfloat16):
    array = jax.random.normal(stream_key, extent, jnp.float32) * deviation
    if len(cuts) > 0:
        array = block_scale(stream_key, extent, cuts, -0.22, 0.18) * array
    return jnp.clip(array, min=-most, max=most).astype(kind)


def setup_inputs(seed: int = 0) -> dict:
    key_of = jax.random.split(jax.random.key(seed), 4)
    saved_input = centred(key_of[0], (HEIGHT, TILE_COLS, CIN), 0.1, 1.5, ((0, 4), (1, 16), (2, 4)))
    upstream = centred(key_of[1], (HEIGHT, TILE_COLS, COUT), 0.25, 4.0, ((0, 4), (2, 16)))
    kernel = centred(key_of[2], (3, 3, CIN, COUT), (9 * CIN) ** -0.5, 0.046875, ((2, 4), (3, 16)))
    return {"saved_input": saved_input, "upstream": upstream, "kernel": kernel}


def shifted_blocks(padded, height, breadth, direction):
    pieces = []
    for step_row in (-1, 0, 1):
        for step_col in (-1, 0, 1):
            top = 1 + direction * step_row
            left = 1 + direction * step_col
            pieces.append(padded[top:top + height, left:left + breadth])
    return jnp.concatenate(pieces, axis=2)


def reference(saved_input, upstream, kernel):
    height, breadth, in_width = saved_input.shape
    out_width = upstream.shape[2]
    block_width = out_width // N_FILT
    active = jnp.maximum(saved_input, jnp.zeros((), jnp.bfloat16))
    padded_grad = jnp.pad(upstream, ((1, 1), (1, 1), (0, 0)))
    stacked_grad = shifted_blocks(padded_grad, height, breadth, -1).reshape(height * breadth, 9, out_width)
    kernel_nine = jnp.transpose(kernel.reshape(9, in_width, out_width), (0, 2, 1))
    active_grad = jnp.zeros((height * breadth, in_width), jnp.float32)
    for block in range(N_FILT):
        low = block * block_width
        grad_piece = stacked_grad[:, :, low:low + block_width].reshape(height * breadth, 9 * block_width)
        kernel_piece = kernel_nine[:, low:low + block_width, :].reshape(9 * block_width, in_width)
        block_grad = jnp.dot(grad_piece, kernel_piece, preferred_element_type=jnp.float32).astype(jnp.bfloat16)
        block_grad = lax.optimization_barrier(block_grad)
        active_grad = active_grad + block_grad.astype(jnp.float32)
    active_grad = active_grad.reshape(height, breadth, in_width)
    input_grad = jnp.where(saved_input > 0, active_grad, jnp.zeros((), jnp.float32)).astype(jnp.bfloat16)
    padded_input = jnp.pad(active, ((1, 1), (1, 1), (0, 0)))
    stacked_input = shifted_blocks(padded_input, height, breadth, 1).reshape(height * breadth, 9 * in_width)
    kernel_grad = jnp.dot(stacked_input.T, upstream.reshape(height * breadth, out_width), preferred_element_type=jnp.float32)
    return input_grad, kernel_grad.reshape(3, 3, in_width, out_width)
```

```python
import jax
import jax.numpy as jnp
from jax import lax
from jax.experimental import pallas as pl
from jax.experimental.pallas import tpu as pltpu
from jax.sharding import PartitionSpec as P

BF16, F32 = jnp.bfloat16, jnp.float32
NY, NZ = 4, 4
UP, DOWN = 0, 1
SIGN = (1, -1)
NEAR = (1, 3)

Z1, Z2 = (0, 1), (2, 3)
Y1 = ((4, 5, 6, 7), (8, 9, 10, 11))
Y2 = ((12, 13, 14, 15), (16, 17, 18, 19))
FAR = ((20, 21), (22, 23))
NR = ((24, 25, 26, 27), (28, 29, 30, 31))
ZF, ZN = (32, 33), (34, 35)
WC, WZ = (36, 37), 38
HALO = (39, 40)
MESSAGES = 41

FAR_BLOCKS = ((2, 1), (3, 0))


def kernel(
    x_ref, u_ref, k_ref, gi_ref, gk_ref,
    kc, uf, s_buf, a_buf, p_buf, far_in, near_in, zfar_in, znear_in,
    wacc, at, wb, wc_in, wz_out, wz_in, halo, ssem, rsem, lsem,
):
    rows, cols, width = u_ref.shape
    chunk = x_ref.shape[0]
    half = chunk // 2
    own_cols = chunk // rows
    group_cols = NZ * own_cols
    taps = 3 * width
    filt, tile = lax.axis_index("filt"), lax.axis_index("tile")
    y, z = lax.div(filt, NZ), lax.rem(filt, NZ)
    lo, core = lax.div(tile, 2), lax.rem(tile, 2)

    def zed(step):
        return lax.rem(z + step, NZ)

    def ycoord(step):
        return lax.rem(y + step, NY)

    def at_y(direction):
        return {"filt": ycoord(NEAR[direction]) * NZ + z}

    def at_z(direction):
        return {"filt": y * NZ + zed(NEAR[direction])}

    def send(number, src, dst, peer):
        return pltpu.make_async_remote_copy(
            src_ref=src, dst_ref=dst, send_sem=ssem.at[number], recv_sem=rsem.at[number],
            device_id=peer, device_id_type=pl.DeviceIdType.MESH,
        )

    started = []

    def start(copy):
        copy.start()
        started.append(copy)

    other_core = {"tile": lo * 2 + 1 - core}
    other_lo = {"tile": (1 - lo) * 2 + core}
    cross = {"tile": (1 - lo) * 2 + 1 - core}

    barrier = pltpu.get_barrier_semaphore()
    peers = [at_y(UP), at_y(DOWN), at_z(UP), at_z(DOWN), other_core, other_lo, cross]
    for peer in peers:
        pl.semaphore_signal(barrier, inc=1, device_id=peer, device_id_type=pl.DeviceIdType.MESH)
    pl.semaphore_wait(barrier, len(peers))

    def halves(direction):
        return pl.ds(direction * half, half)

    def z1(d):
        return send(Z1[d], x_ref, a_buf.at[0, z], at_z(d))

    def z2(d):
        slot = a_buf.at[0, zed(NEAR[1 - d]), halves(d)]
        return send(Z2[d], slot, slot, at_z(d))

    def y1(d, b):
        src = x_ref if b == 0 else a_buf.at[0, zed(b)]
        return send(Y1[d][b], src, a_buf.at[NEAR[1 - d], zed(b)], at_y(d))

    def y2(d, b):
        return send(
            Y2[d][b], a_buf.at[NEAR[1 - d], zed(b), halves(d)], a_buf.at[2, zed(b), halves(d)], at_y(d)
        )

    def far(d, k):
        return send(FAR[d][k], p_buf.at[2, zed(FAR_BLOCKS[d][k])], far_in.at[d, k], at_y(d))

    def near(d, b):
        return send(NR[d][b], p_buf.at[NEAR[d], zed(b)], near_in.at[d, b], at_y(d))

    def zfar(d):
        return send(ZF[d], p_buf.at[0, zed(2), halves(d)], zfar_in.at[d], at_z(d))

    def znear(d):
        return send(ZN[d], p_buf.at[0, zed(NEAR[d])], znear_in.at[d], at_z(d))

    def wcore(k):
        return send(WC[k], wb.at[2 * k + 1 - core], wc_in.at[k], other_core)

    def wlo():
        return send(WZ, wz_out, wz_in, other_lo)

    def halo_down():
        return send(HALO[0], u_ref.at[0], halo.at[1], {"tile": tile - 1})

    def halo_up():
        return send(HALO[1], u_ref.at[rows - 1], halo.at[0], {"tile": tile + 1})

    first, last = tile == 0, tile == 3

    for d in (UP, DOWN):
        start(z1(d))
        start(y1(d, 0))

    @pl.when(jnp.logical_not(first))
    def _():
        halo_down().start()

    @pl.when(jnp.logical_not(last))
    def _():
        halo_up().start()

    own = pltpu.make_async_copy(x_ref, a_buf.at[0, z], lsem.at[9])
    own.start()
    weights = []
    for si in range(3):
        for ri in range(3):
            place = si * 3 + ri
            copy = pltpu.make_async_copy(
                k_ref.at[ri * 3 + si], kc.at[:, pl.ds(place * width, width)], lsem.at[place]
            )
            copy.start()
            weights.append(copy)

    @pl.loop(0, rows)
    def _(i):
        uf[pl.ds(pl.multiple_of((i + 1) * cols, 8), cols), :] = u_ref[i].astype(F32)

    s_buf[1, :, 2 * taps :] = jnp.zeros((rows, taps), BF16)
    s_buf[cols, :, :taps] = jnp.zeros((rows, taps), BF16)

    @pl.when(first)
    def _():
        uf[:cols, :] = jnp.zeros((cols, width), F32)

    @pl.when(jnp.logical_not(first))
    def _():
        halo_up().wait_recv()
        uf[:cols, :] = halo[0].astype(F32)

    bottom = (rows + 1) * cols

    @pl.when(last)
    def _():
        uf[bottom:, :] = jnp.zeros((cols, width), F32)

    @pl.when(jnp.logical_not(last))
    def _():
        halo_down().wait_recv()
        uf[bottom:, :] = halo[1].astype(F32)

    @pl.loop(0, cols)
    def _(j):
        for ri in range(3):
            value = uf[pl.ds((2 - ri) * cols + j, rows, stride=cols), :].astype(BF16)
            for si in range(3):
                s_buf[j + si, :, pl.ds(si * taps + ri * width, width)] = value

    for copy in weights:
        copy.wait()

    def stacked(a):
        block = s_buf[pl.ds(ycoord(a) * group_cols + 1, group_cols)]
        return block.reshape(NZ * chunk, 3 * taps)

    def dgrad(a):
        part = lax.dot_general(
            stacked(a), kc[...], (((1,), (1,)), ((), ())), preferred_element_type=F32
        )
        p_buf[a] = part.astype(BF16).reshape(NZ, chunk, part.shape[1])

    def wgrad(a):
        chunks = a_buf[a].reshape(NZ * chunk, a_buf.shape[3])
        at[...] = jnp.maximum(chunks, jnp.zeros((), BF16)).T
        part = jnp.dot(at[...], stacked(a), preferred_element_type=F32).reshape(wacc.shape)
        if a == 0:
            wacc[...] = part
        else:
            wacc[...] += part

    def add_far(d, k):
        slot = (NEAR[d], zed(FAR_BLOCKS[d][k]))
        far(d, k).wait_recv()
        p_buf[slot] = (p_buf[slot].astype(F32) + far_in[d, k].astype(F32)).astype(BF16)

    def near_sum(b):
        near(UP, b).wait_recv()
        near(DOWN, b).wait_recv()
        return p_buf[0, zed(b)].astype(F32) + near_in[UP, b].astype(F32) + near_in[DOWN, b].astype(F32)

    dgrad(2)
    for k in (0, 1):
        for d in (UP, DOWN):
            start(far(d, k))
    dgrad(1)
    dgrad(3)
    for d in (UP, DOWN):
        z1(d).wait_recv()
        b = NEAR[1 - d]
        start(z2(d))
        start(y1(UP, b))
        start(y1(DOWN, b))
    for d in (UP, DOWN):
        y1(d, 0).wait_recv()
        start(y2(d, 0))
    dgrad(0)
    add_far(UP, 0)
    start(near(UP, 2))
    start(near(DOWN, 2))
    for d in (UP, DOWN):
        z2(d).wait_recv()
    for d in (UP, DOWN):
        start(y1(d, 2))
    own.wait()
    wgrad(0)
    for b in (3, 1):
        for d in (UP, DOWN):
            y1(d, b).wait_recv()
            start(y2(d, b))
    for d in (UP, DOWN):
        y1(d, 2).wait_recv()
        start(y2(d, 2))
    add_far(UP, 1)
    start(near(UP, 1))
    start(near(DOWN, 1))
    add_far(DOWN, 0)
    start(near(UP, 3))
    start(near(DOWN, 3))
    add_far(DOWN, 1)
    start(near(UP, 0))
    start(near(DOWN, 0))
    wgrad(3)
    wgrad(1)
    p_buf[0, zed(2)] = near_sum(2).astype(BF16)
    for d in (UP, DOWN):
        start(zfar(d))
    for b in range(NZ):
        for d in (UP, DOWN):
            y2(d, b).wait_recv()
    wgrad(2)
    wb[...] = wacc[...].astype(BF16)
    for k in (0, 1):
        start(wcore(k))
    for d in (UP, DOWN):
        b = NEAR[d]
        total = near_sum(b)
        zfar(d).wait_recv()
        p_buf[0, zed(b)] = total.astype(BF16)
        p_buf[0, zed(b), halves(d)] = (
            total[d * half : (d + 1) * half] + zfar_in[d].astype(F32)
        ).astype(BF16)
        start(znear(d))
    for k in (0, 1):
        wcore(k).wait_recv()
    wz_out[...] = (wacc[2 * (1 - lo) + core] + wc_in[1 - lo].astype(F32)).astype(BF16)
    start(wlo())
    total = near_sum(0)
    for d in (UP, DOWN):
        znear(d).wait_recv()
    total += znear_in[UP].astype(F32) + znear_in[DOWN].astype(F32)
    gi_ref[...] = jnp.where(x_ref[...] > 0, total, 0.0).astype(BF16)
    wlo().wait_recv()
    grad = wacc[tile] + wc_in[lo].astype(F32) + wz_in[...].astype(F32)
    for si in range(3):
        for ri in range(3):
            place = (si * 3 + ri) * width
            gk_ref[ri * 3 + si] = grad[:, place : place + width]
    for copy in started:
        copy.wait_send()

    @pl.when(jnp.logical_not(first))
    def _():
        halo_down().wait_send()

    @pl.when(jnp.logical_not(last))
    def _():
        halo_up().wait_send()


def per_device(saved_input, upstream, weights):
    rows, cols, width = upstream.shape
    own_cols, channels = saved_input.shape[1], saved_input.shape[2]
    chunk = own_cols * rows
    half = chunk // 2
    x = jnp.transpose(saved_input, (1, 0, 2)).reshape(chunk, channels)
    vmem = pl.BlockSpec(memory_space=pltpu.VMEM)
    block = channels // 4
    gi, gk = pl.pallas_call(
        kernel,
        name="conv_backward",
        out_shape=(
            jax.ShapeDtypeStruct((chunk, channels), BF16),
            jax.ShapeDtypeStruct((9, block, width), F32),
        ),
        in_specs=[vmem, vmem, pl.BlockSpec(memory_space=pl.ANY)],
        out_specs=(vmem, vmem),
        scratch_shapes=[
            pltpu.VMEM((channels, 9 * width), BF16),
            pltpu.VMEM(((rows + 2) * cols, width), F32),
            pltpu.VMEM((cols + 2, rows, 9 * width), BF16),
            pltpu.VMEM((NY, NZ, chunk, channels), BF16),
            pltpu.VMEM((NY, NZ, chunk, channels), BF16),
            pltpu.VMEM((2, 2, chunk, channels), BF16),
            pltpu.VMEM((2, NZ, chunk, channels), BF16),
            pltpu.VMEM((2, half, channels), BF16),
            pltpu.VMEM((2, chunk, channels), BF16),
            pltpu.VMEM((4, block, 9 * width), F32),
            pltpu.VMEM((channels, NZ * chunk), BF16),
            pltpu.VMEM((4, block, 9 * width), BF16),
            pltpu.VMEM((2, block, 9 * width), BF16),
            pltpu.VMEM((block, 9 * width), BF16),
            pltpu.VMEM((block, 9 * width), BF16),
            pltpu.VMEM((2, cols, width), BF16),
            pltpu.SemaphoreType.DMA((MESSAGES,)),
            pltpu.SemaphoreType.DMA((MESSAGES,)),
            pltpu.SemaphoreType.DMA((10,)),
        ],
        compiler_params=pltpu.CompilerParams(
            collective_id=0, has_side_effects=True, vmem_limit_bytes=60 * 1024 * 1024
        ),
    )(x, upstream, weights.reshape(9, channels, width))
    input_grad = jnp.transpose(gi.reshape(own_cols, rows, channels), (1, 0, 2))
    return input_grad, gk.reshape(3, 3, block, width)


def solution(mesh):
    placed = (P("tile", "filt", "chan"), P("tile", None, "filt"), P(None, None, "chan", "filt"))
    return jax.shard_map(
        per_device,
        mesh=mesh,
        in_specs=placed,
        out_specs=(P("tile", "filt", "chan"), P(None, None, ("chan", "tile"), "filt")),
        check_vma=False,
    )
```

```python
from contextlib import nullcontext as mark

import jax
import jax.numpy as jnp
from jax import lax
from jax.experimental import pallas as pl
from jax.experimental.pallas import tpu as pltpu
from jax.sharding import PartitionSpec as P

BF16, F32 = jnp.bfloat16, jnp.float32
NY, NZ = 4, 4
UP, DOWN = 0, 1
BOTH = (UP, DOWN)
NEAR = (1, 3)
FAR_BLOCKS = ((2, 1), (3, 0))
Z_ROWS = 64


class Numbers:
    def __init__(self):
        self.known = {}

    def __call__(self, *key):
        return self.known.setdefault(key, len(self.known))


MESSAGES = 80


def kernel(
    x_ref, u_ref, k_ref, gi_ref, gk_ref,
    u_vm, kc, uf, s_buf, a_buf, p_buf, far_y, near_y, far_z, near_z, far2_y, near2_y, far2_z, near2_z,
    wacc, at, wb, wc_in, wz_out, wz_in, halo, ssem, rsem, lsem,
):
    rows, cols, width = u_ref.shape
    chunk = x_ref.shape[0]
    half = chunk // 2
    own_cols = chunk // rows
    group_cols = NZ * own_cols
    taps = 3 * width
    filt, tile = lax.axis_index("filt"), lax.axis_index("tile")
    y, z = lax.div(filt, NZ), lax.rem(filt, NZ)
    lo, core = lax.div(tile, 2), lax.rem(tile, 2)
    number = Numbers()

    def zed(step):
        return lax.rem(z + step, NZ)

    def ycoord(step):
        return lax.rem(y + step, NY)

    def at_y(direction):
        return {"filt": ycoord(NEAR[direction]) * NZ + z}

    def at_z(direction):
        return {"filt": y * NZ + zed(NEAR[direction])}

    def send(key, src, dst, peer):
        n = number(*key)
        return pltpu.make_async_remote_copy(
            src_ref=src, dst_ref=dst, send_sem=ssem.at[n], recv_sem=rsem.at[n],
            device_id=peer, device_id_type=pl.DeviceIdType.MESH,
        )

    started = []

    def start(copy):
        copy.start()
        started.append(copy)

    other_core = {"tile": lo * 2 + 1 - core}
    other_lo = {"tile": (1 - lo) * 2 + core}
    cross = {"tile": (1 - lo) * 2 + 1 - core}

    barrier = pltpu.get_barrier_semaphore()
    peers = [at_y(UP), at_y(DOWN), at_z(UP), at_z(DOWN), other_core, other_lo, cross]
    for peer in peers:
        pl.semaphore_signal(barrier, inc=1, device_id=peer, device_id_type=pl.DeviceIdType.MESH)

    upstream_copy = pltpu.make_async_copy(u_ref, u_vm, lsem.at[10])
    upstream_copy.start()
    own = pltpu.make_async_copy(x_ref, a_buf.at[0, z], lsem.at[9])
    own.start()
    weights = []
    for si in range(3):
        for ri in range(3):
            place = si * 3 + ri
            copy = pltpu.make_async_copy(
                k_ref.at[ri * 3 + si], kc.at[:, pl.ds(place * width, width)], lsem.at[place]
            )
            copy.start()
            weights.append(copy)
    with mark("a_barrier"):
        pl.semaphore_wait(barrier, len(peers))

    def part(h):
        return pl.ds(h * half, half)

    def z1(d, h):
        return send(("z1", d, h), x_ref.at[part(h)], a_buf.at[0, z, part(h)], at_z(d))

    def z2(d):
        slot = a_buf.at[0, zed(NEAR[1 - d]), part(d)]
        return send(("z2", d), slot, slot, at_z(d))

    def y1(d, b, h):
        src = x_ref.at[part(h)] if b == 0 else a_buf.at[0, zed(b), part(h)]
        return send(("y1", d, b, h), src, a_buf.at[NEAR[1 - d], zed(b), part(h)], at_y(d))

    def y2(d, b):
        return send(
            ("y2", d, b), a_buf.at[NEAR[1 - d], zed(b), part(d)], a_buf.at[2, zed(b), part(d)], at_y(d)
        )

    def wcore(k):
        return send(("wc", k), wb.at[2 * k + 1 - core], wc_in.at[k], other_core)

    def wlo():
        return send(("wz",), wz_out, wz_in, other_lo)

    def halo_down():
        return send(("halo", 0), u_ref.at[0], halo.at[1], {"tile": tile - 1})

    def halo_up():
        return send(("halo", 1), u_ref.at[rows - 1], halo.at[0], {"tile": tile + 1})

    class Reduce:
        def __init__(self, name, low, count, first, second, swap, bufs):
            self.name, self.low, self.count = name, low, count
            self.first, self.second, self.swap = first, second, swap
            self.far_in, self.near_in, self.far2_in, self.near2_in = bufs

        def block(self, i, j, h=None):
            low, count = self.low, self.count
            if h is not None:
                count //= 2
                low += h * count
            slot = (j, i) if self.swap else (i, j)
            return (*slot, pl.ds(low, count))

        def far(self, d, k):
            src = p_buf.at[self.block(2, FAR_BLOCKS[d][k])]
            return send((self.name, "far", d, k), src, self.far_in.at[d, k], self.first(d))

        def near(self, d, b):
            src = p_buf.at[self.block(NEAR[d], b)]
            return send((self.name, "near", d, b), src, self.near_in.at[d, b], self.first(d))

        def far2(self, d):
            src = p_buf.at[self.block(0, 2, d)]
            return send((self.name, "far2", d), src, self.far2_in.at[d], self.second(d))

        def near2(self, d):
            src = p_buf.at[self.block(0, NEAR[d])]
            return send((self.name, "near2", d), src, self.near2_in.at[d], self.second(d))

        def send_far(self, k):
            for d in BOTH:
                start(self.far(d, k))

        def send_near(self, b):
            d, k = {2: (UP, 0), 1: (UP, 1), 3: (DOWN, 0), 0: (DOWN, 1)}[b]
            start(self.near(1 - d, b))
            self.far(d, k).wait_recv()
            slot = self.block(NEAR[d], b)
            p_buf[slot] = (p_buf[slot].astype(F32) + self.far_in[d, k].astype(F32)).astype(BF16)
            start(self.near(d, b))

        def near_sum(self, b):
            for d in BOTH:
                self.near(d, b).wait_recv()
            own_term = p_buf[self.block(0, b)].astype(F32)
            return own_term + self.near_in[UP, b].astype(F32) + self.near_in[DOWN, b].astype(F32)

        def send_far2(self):
            p_buf[self.block(0, 2)] = self.near_sum(2).astype(BF16)
            for d in BOTH:
                start(self.far2(d))

        def send_near2(self, d):
            b, n = NEAR[d], self.count // 2
            total = self.near_sum(b)
            self.far2(d).wait_recv()
            p_buf[self.block(0, b, 1 - d)] = total[(1 - d) * n : (2 - d) * n].astype(BF16)
            p_buf[self.block(0, b, d)] = (
                total[d * n : (d + 1) * n] + self.far2_in[d].astype(F32)
            ).astype(BF16)
            start(self.near2(d))

        def finish(self):
            total = self.near_sum(0)
            for d in BOTH:
                self.near2(d).wait_recv()
            total += self.near2_in[UP].astype(F32) + self.near2_in[DOWN].astype(F32)
            place = pl.ds(self.low, self.count)
            gi_ref[place] = jnp.where(a_buf[0, z, place] > 0, total, 0.0).astype(BF16)

    red_z = Reduce("rz", 0, Z_ROWS, at_z, at_y, True, (far_z, near_z, far2_z, near2_z))
    red_y = Reduce("ry", Z_ROWS, chunk - Z_ROWS, at_y, at_z, False, (far_y, near_y, far2_y, near2_y))

    first, last = tile == 0, tile == 3

    @pl.when(jnp.logical_not(first))
    def _():
        halo_down().start()

    @pl.when(jnp.logical_not(last))
    def _():
        halo_up().start()

    for h in BOTH:
        for d in BOTH:
            start(z1(d, h ^ d))
            start(y1(d, 0, h ^ d))

    with mark("b_uf"):
        upstream_copy.wait()

        @pl.loop(0, rows)
        def _(i):
            uf[pl.ds(pl.multiple_of((i + 1) * cols, 8), cols), :] = u_vm[i].astype(F32)

    s_buf[1, :, 2 * taps :] = jnp.zeros((rows, taps), BF16)
    s_buf[cols, :, :taps] = jnp.zeros((rows, taps), BF16)
    bottom = (rows + 1) * cols
    with mark("c_halo"):

        @pl.when(first)
        def _():
            uf[:cols, :] = jnp.zeros((cols, width), F32)

        @pl.when(jnp.logical_not(first))
        def _():
            halo_up().wait_recv()
            uf[:cols, :] = halo[0].astype(F32)

        @pl.when(last)
        def _():
            uf[bottom:, :] = jnp.zeros((cols, width), F32)

        @pl.when(jnp.logical_not(last))
        def _():
            halo_down().wait_recv()
            uf[bottom:, :] = halo[1].astype(F32)

    with mark("d_im2col"):

        @pl.loop(0, cols)
        def _(j):
            for ri in range(3):
                value = uf[pl.ds((2 - ri) * cols + j, rows, stride=cols), :].astype(BF16)
                for si in range(3):
                    s_buf[j + si, :, pl.ds(si * taps + ri * width, width)] = value

        for copy in weights:
            copy.wait()

    def stacked(a):
        block = s_buf[pl.ds(ycoord(a) * group_cols + 1, group_cols)]
        return block.reshape(NZ * chunk, 3 * taps)

    def dgrad(a):
        with mark(f"dgrad{a}"):
            value = lax.dot_general(
                stacked(a), kc[...], (((1,), (1,)), ((), ())), preferred_element_type=F32
            ).astype(BF16)
            for place in range(NZ):
                p_buf[a, lax.rem(place - z + NZ, NZ)] = value[place * chunk : (place + 1) * chunk]

    def wgrad(a):
        with mark(f"wgrad{a}"):
            chunks = a_buf[a].reshape(NZ * chunk, a_buf.shape[3])
            at[...] = jnp.maximum(chunks, jnp.zeros((), BF16)).T
            value = jnp.dot(at[...], stacked(a), preferred_element_type=F32).reshape(wacc.shape)
            if a == 0:
                wacc[...] = value
            else:
                wacc[...] += value

    def pass_y(d, b):
        y1(d, b, d).wait_recv()
        start(y2(d, b))

    dgrad(2)
    with mark("01_z1_first"):
        for d in BOTH:
            z1(d, d).wait_recv()
            start(z2(d))
            for e in BOTH:
                start(y1(e, NEAR[1 - d], d))
        for d in BOTH:
            pass_y(d, 0)
    dgrad(1)
    dgrad(3)
    dgrad(0)
    with mark("02_z1_second"):
        for d in BOTH:
            z1(d, 1 - d).wait_recv()
            for e in BOTH:
                start(y1(e, NEAR[1 - d], 1 - d))
        for k in (0, 1):
            red_z.send_far(k)
    with mark("03_pass_first"):
        for d in BOTH:
            pass_y(d, NEAR[1 - d])
        for k in (0, 1):
            red_y.send_far(k)
    own.wait()
    with mark("04_z2"):
        for d in BOTH:
            z2(d).wait_recv()
            for e in BOTH:
                start(y1(e, 2, d))
    wgrad(0)
    with mark("05_pass_second"):
        for d in BOTH:
            pass_y(d, NEAR[d])
    with mark("06_rz_near"):
        for b in (2, 1, 3, 0):
            red_z.send_near(b)
    with mark("07_pass_far"):
        for d in BOTH:
            pass_y(d, 2)
    with mark("08_ry_near_21"):
        for b in (2, 1):
            red_y.send_near(b)
    with mark("09_rz_far2"):
        red_z.send_far2()
    with mark("10_y1_rest"):
        for b in range(NZ):
            for d in BOTH:
                y1(d, b, 1 - d).wait_recv()
    wgrad(3)
    wgrad(1)
    with mark("11_ry_near_30"):
        for b in (3, 0):
            red_y.send_near(b)
    with mark("12_rz_near2"):
        for d in BOTH:
            red_z.send_near2(d)
    with mark("13_y2"):
        for b in range(NZ):
            for d in BOTH:
                y2(d, b).wait_recv()
    wgrad(2)
    with mark("14_wcore"):
        wb[...] = wacc[...].astype(BF16)
        for k in (0, 1):
            start(wcore(k))
    with mark("15_ry_far2"):
        red_y.send_far2()
    with mark("16_wcore_in"):
        for k in (0, 1):
            wcore(k).wait_recv()
        wz_out[...] = (wacc[2 * (1 - lo) + core] + wc_in[1 - lo].astype(F32)).astype(BF16)
        start(wlo())
    with mark("17_ry_near2"):
        for d in BOTH:
            red_y.send_near2(d)
    with mark("18_rz_finish"):
        red_z.finish()
    with mark("19_ry_finish"):
        red_y.finish()
    with mark("20_wlo_in"):
        wlo().wait_recv()
        grad = wacc[tile] + wc_in[lo].astype(F32) + wz_in[...].astype(F32)
        for si in range(3):
            for ri in range(3):
                place = (si * 3 + ri) * width
                gk_ref[ri * 3 + si] = grad[:, place : place + width]
    with mark("21_sends"):
        for copy in started:
            copy.wait_send()

        @pl.when(jnp.logical_not(first))
        def _():
            halo_down().wait_send()

        @pl.when(jnp.logical_not(last))
        def _():
            halo_up().wait_send()


def write_out(gi_ref, gk_ref, gi_out, gk_out, sem):
    copies = [
        pltpu.make_async_copy(gi_ref, gi_out, sem.at[0]),
        pltpu.make_async_copy(gk_ref, gk_out, sem.at[1]),
    ]
    for copy in copies:
        copy.start()
    for copy in copies:
        copy.wait()


def per_device(saved_input, upstream, weights):
    rows, cols, width = upstream.shape
    own_cols, channels = saved_input.shape[1], saved_input.shape[2]
    chunk = own_cols * rows
    x = jnp.transpose(saved_input, (1, 0, 2)).reshape(chunk, channels)
    hbm = pl.BlockSpec(memory_space=pl.ANY)
    vmem = pl.BlockSpec(memory_space=pltpu.VMEM)
    block = channels // 4
    y_rows = chunk - Z_ROWS
    gi_shape, gk_shape = (chunk, channels), (9, block, width)

    def landing(n):
        return [
            pltpu.VMEM((2, 2, n, channels), BF16),
            pltpu.VMEM((2, NZ, n, channels), BF16),
        ]

    def landing2(n):
        return [pltpu.VMEM((2, n // 2, channels), BF16), pltpu.VMEM((2, n, channels), BF16)]

    gi, gk = pl.pallas_call(
        kernel,
        name="conv_backward",
        out_shape=(pltpu.VMEM(gi_shape, BF16), pltpu.VMEM(gk_shape, F32)),
        in_specs=[hbm, hbm, hbm],
        out_specs=(vmem, vmem),
        scratch_shapes=[
            pltpu.VMEM((rows, cols, width), BF16),
            pltpu.VMEM((channels, 9 * width), BF16),
            pltpu.VMEM(((rows + 2) * cols, width), F32),
            pltpu.VMEM((cols + 2, rows, 9 * width), BF16),
            pltpu.VMEM((NY, NZ, chunk, channels), BF16),
            pltpu.VMEM((NY, NZ, chunk, channels), BF16),
            *landing(y_rows),
            *landing(Z_ROWS),
            *landing2(y_rows),
            *landing2(Z_ROWS),
            pltpu.VMEM((4, block, 9 * width), F32),
            pltpu.VMEM((channels, NZ * chunk), BF16),
            pltpu.VMEM((4, block, 9 * width), BF16),
            pltpu.VMEM((2, block, 9 * width), BF16),
            pltpu.VMEM((block, 9 * width), BF16),
            pltpu.VMEM((block, 9 * width), BF16),
            pltpu.VMEM((2, cols, width), BF16),
            pltpu.SemaphoreType.DMA((MESSAGES,)),
            pltpu.SemaphoreType.DMA((MESSAGES,)),
            pltpu.SemaphoreType.DMA((11,)),
        ],
        compiler_params=pltpu.CompilerParams(
            collective_id=0, has_side_effects=True, vmem_limit_bytes=56 * 1024 * 1024
        ),
    )(x, upstream, weights.reshape(9, channels, width))
    gi, gk = pl.pallas_call(
        write_out,
        name="write_out",
        out_shape=(jax.ShapeDtypeStruct(gi_shape, BF16), jax.ShapeDtypeStruct(gk_shape, F32)),
        in_specs=[vmem, vmem],
        out_specs=(hbm, hbm),
        scratch_shapes=[pltpu.SemaphoreType.DMA((2,))],
        compiler_params=pltpu.CompilerParams(vmem_limit_bytes=1024 * 1024),
    )(gi, gk)
    input_grad = jnp.transpose(gi.reshape(own_cols, rows, channels), (1, 0, 2))
    return input_grad, gk.reshape(3, 3, block, width)


def solution(mesh):
    placed = (P("tile", "filt", "chan"), P("tile", None, "filt"), P(None, None, "chan", "filt"))
    return jax.shard_map(
        per_device,
        mesh=mesh,
        in_specs=placed,
        out_specs=(P("tile", "filt", "chan"), P(None, None, ("chan", "tile"), "filt")),
        check_vma=False,
    )
```

```python
import functools
from contextlib import nullcontext as mark

import jax
import jax.numpy as jnp
from jax import lax
from jax.experimental import pallas as pl
from jax.experimental.pallas import tpu as pltpu
from jax.sharding import PartitionSpec as P

BF16, F32 = jnp.bfloat16, jnp.float32
NY, NZ = 4, 4
UP, DOWN = 0, 1
BOTH = (UP, DOWN)
NEAR = (1, 3)
FAR_BLOCKS = ((2, 1), (3, 0))
RELAY = {2: (UP, 0), 1: (UP, 1), 3: (DOWN, 0), 0: (DOWN, 1)}
Z_ROWS = 96


class Numbers:
    def __init__(self):
        self.known = {}

    def __call__(self, *key):
        return self.known.setdefault(key, len(self.known))


MESSAGES = 67

ORDER = (
    "pass00", "dgrad2", "ry_far10", "z1a1", "z1a0", "dgrad1",
    "ry_far01", "dgrad0", "dgrad3", "rz_dir0", "rz_far01", "ry_dir2",
    "rz_dir1", "rz_far11", "ry_far00", "z2_1", "z1b0", "ry_dir1",
    "pass11", "z2_0", "rz_far00", "rz_far10", "pass03", "ry_dep3",
    "z1b1", "ry_dep2", "pass12", "ry_dir3", "pass13", "rz_dir2",
    "rz_dep2", "wgrad0", "pass02", "ry_dep1", "rz_dep0", "rz_dir3",
    "pass01", "pass10", "ry_far2", "wgrad1", "rz_dep3", "rz_dep1",
    "rz_far2", "wgrad3", "ry_near21", "ry_near20", "ry_far11", "wgrad2",
    "wcore", "rz_near20", "wlo", "rz_near21", "ry_dir0", "ry_dep0",
    "ry_fin", "rz_fin", "wfin",
)


def kernel(
    x_ref, u_ref, k_ref, gi_ref, gk_ref,
    u_vm, kc, uf, s_buf, a_buf, p_buf, far_y, near_y, far_z, near_z, far2_y, near2_y, far2_z, near2_z,
    wacc, at, wb, wc_in, wz_out, wz_in, halo, ssem, rsem, lsem,
):
    rows, cols, width = u_ref.shape
    chunk = x_ref.shape[0]
    half = chunk // 2
    own_cols = chunk // rows
    group_cols = NZ * own_cols
    taps = 3 * width
    filt, tile = lax.axis_index("filt"), lax.axis_index("tile")
    y, z = lax.div(filt, NZ), lax.rem(filt, NZ)
    lo, core = lax.div(tile, 2), lax.rem(tile, 2)
    number = Numbers()

    def zed(step):
        return lax.rem(z + step, NZ)

    def ycoord(step):
        return lax.rem(y + step, NY)

    def at_y(direction):
        return {"filt": ycoord(NEAR[direction]) * NZ + z}

    def at_z(direction):
        return {"filt": y * NZ + zed(NEAR[direction])}

    def send(key, src, dst, peer):
        n = number(*key)
        return pltpu.make_async_remote_copy(
            src_ref=src, dst_ref=dst, send_sem=ssem.at[n], recv_sem=rsem.at[n],
            device_id=peer, device_id_type=pl.DeviceIdType.MESH,
        )

    started = []

    def start(copy):
        copy.start()
        started.append(copy)

    other_core = {"tile": lo * 2 + 1 - core}
    other_lo = {"tile": (1 - lo) * 2 + core}
    cross = {"tile": (1 - lo) * 2 + 1 - core}

    barrier = pltpu.get_barrier_semaphore()
    peers = [at_y(UP), at_y(DOWN), at_z(UP), at_z(DOWN), other_core, other_lo, cross]
    for peer in peers:
        pl.semaphore_signal(barrier, inc=1, device_id=peer, device_id_type=pl.DeviceIdType.MESH)

    upstream_copy = pltpu.make_async_copy(u_ref, u_vm, lsem.at[10])
    upstream_copy.start()
    own = pltpu.make_async_copy(x_ref, a_buf.at[0, z], lsem.at[9])
    own.start()
    weights = []
    for si in range(3):
        for ri in range(3):
            place = si * 3 + ri
            copy = pltpu.make_async_copy(
                k_ref.at[ri * 3 + si], kc.at[:, pl.ds(place * width, width)], lsem.at[place]
            )
            copy.start()
            weights.append(copy)
    with mark("a_barrier"):
        pl.semaphore_wait(barrier, len(peers))

    def part(h):
        return pl.ds(h * half, half)

    def z1(d, h):
        return send(("z1", d, h), x_ref.at[part(h)], a_buf.at[0, z, part(h)], at_z(d))

    def z2(d):
        slot = a_buf.at[0, zed(NEAR[1 - d]), part(d)]
        return send(("z2", d), slot, slot, at_z(d))

    def y1(d, b, h):
        src = x_ref.at[part(h)] if b == 0 else a_buf.at[0, zed(b), part(h)]
        return send(("y1", d, b, h), src, a_buf.at[NEAR[1 - d], zed(b), part(h)], at_y(d))

    def y2(d, b):
        return send(
            ("y2", d, b), a_buf.at[NEAR[1 - d], zed(b), part(d)], a_buf.at[2, zed(b), part(d)], at_y(d)
        )

    def wcore(k):
        return send(("wc", k), wb.at[2 * k + 1 - core], wc_in.at[k], other_core)

    def wlo():
        return send(("wz",), wz_out, wz_in, other_lo)

    def halo_down():
        return send(("halo", 0), u_ref.at[0], halo.at[1], {"tile": tile - 1})

    def halo_up():
        return send(("halo", 1), u_ref.at[rows - 1], halo.at[0], {"tile": tile + 1})

    class Reduce:
        def __init__(self, name, low, count, first, second, swap, bufs):
            self.name, self.low, self.count = name, low, count
            self.first, self.second, self.swap = first, second, swap
            self.far_in, self.near_in, self.far2_in, self.near2_in = bufs

        def block(self, i, j, h=None):
            low, count = self.low, self.count
            if h is not None:
                count //= 2
                low += h * count
            slot = (j, i) if self.swap else (i, j)
            return (*slot, pl.ds(low, count))

        def far(self, d, k):
            src = p_buf.at[self.block(2, FAR_BLOCKS[d][k])]
            return send((self.name, "far", d, k), src, self.far_in.at[d, k], self.first(d))

        def near(self, d, b):
            src = p_buf.at[self.block(NEAR[d], b)]
            return send((self.name, "near", d, b), src, self.near_in.at[d, b], self.first(d))

        def far2(self, d):
            src = p_buf.at[self.block(0, 2, d)]
            return send((self.name, "far2", d), src, self.far2_in.at[d], self.second(d))

        def near2(self, d):
            src = p_buf.at[self.block(0, NEAR[d])]
            return send((self.name, "near2", d), src, self.near2_in.at[d], self.second(d))

        def send_far(self, d, k):
            start(self.far(d, k))

        def send_direct(self, b):
            start(self.near(1 - RELAY[b][0], b))

        def send_relayed(self, b):
            d, k = RELAY[b]
            self.far(d, k).wait_recv()
            slot = self.block(NEAR[d], b)
            p_buf[slot] = (p_buf[slot].astype(F32) + self.far_in[d, k].astype(F32)).astype(BF16)
            start(self.near(d, b))

        def near_sum(self, b):
            for d in BOTH:
                self.near(d, b).wait_recv()
            own_term = p_buf[self.block(0, b)].astype(F32)
            return own_term + self.near_in[UP, b].astype(F32) + self.near_in[DOWN, b].astype(F32)

        def send_far2(self):
            p_buf[self.block(0, 2)] = self.near_sum(2).astype(BF16)
            for d in BOTH:
                start(self.far2(d))

        def send_near2(self, d):
            b, n = NEAR[d], self.count // 2
            total = self.near_sum(b)
            self.far2(d).wait_recv()
            p_buf[self.block(0, b, 1 - d)] = total[(1 - d) * n : (2 - d) * n].astype(BF16)
            p_buf[self.block(0, b, d)] = (
                total[d * n : (d + 1) * n] + self.far2_in[d].astype(F32)
            ).astype(BF16)
            start(self.near2(d))

        def finish(self):
            total = self.near_sum(0)
            for d in BOTH:
                self.near2(d).wait_recv()
            total += self.near2_in[UP].astype(F32) + self.near2_in[DOWN].astype(F32)
            place = pl.ds(self.low, self.count)
            gi_ref[place] = jnp.where(a_buf[0, z, place] > 0, total, 0.0).astype(BF16)

    red_z = Reduce("rz", 0, Z_ROWS, at_z, at_y, True, (far_z, near_z, far2_z, near2_z))
    red_y = Reduce("ry", Z_ROWS, chunk - Z_ROWS, at_y, at_z, False, (far_y, near_y, far2_y, near2_y))

    first, last = tile == 0, tile == 3

    @pl.when(jnp.logical_not(first))
    def _():
        halo_down().start()

    @pl.when(jnp.logical_not(last))
    def _():
        halo_up().start()

    for h in BOTH:
        for d in BOTH:
            start(z1(d, h ^ d))
            start(y1(d, 0, h ^ d))

    with mark("b_uf"):
        upstream_copy.wait()

        @pl.loop(0, rows)
        def _(i):
            uf[pl.ds(pl.multiple_of((i + 1) * cols, 8), cols), :] = u_vm[i].astype(F32)

    s_buf[1, :, 2 * taps :] = jnp.zeros((rows, taps), BF16)
    s_buf[cols, :, :taps] = jnp.zeros((rows, taps), BF16)
    bottom = (rows + 1) * cols
    with mark("c_halo"):

        @pl.when(first)
        def _():
            uf[:cols, :] = jnp.zeros((cols, width), F32)

        @pl.when(jnp.logical_not(first))
        def _():
            halo_up().wait_recv()
            uf[:cols, :] = halo[0].astype(F32)

        @pl.when(last)
        def _():
            uf[bottom:, :] = jnp.zeros((cols, width), F32)

        @pl.when(jnp.logical_not(last))
        def _():
            halo_down().wait_recv()
            uf[bottom:, :] = halo[1].astype(F32)

    with mark("d_im2col"):

        @pl.loop(0, cols)
        def _(j):
            for ri in range(3):
                value = uf[pl.ds((2 - ri) * cols + j, rows, stride=cols), :].astype(BF16)
                for si in range(3):
                    s_buf[j + si, :, pl.ds(si * taps + ri * width, width)] = value

        for copy in weights:
            copy.wait()

    def stacked(a):
        block = s_buf[pl.ds(ycoord(a) * group_cols + 1, group_cols)]
        return block.reshape(NZ * chunk, 3 * taps)

    def dgrad(a):
        value = lax.dot_general(
            stacked(a), kc[...], (((1,), (1,)), ((), ())), preferred_element_type=F32
        ).astype(BF16)
        for place in range(NZ):
            p_buf[a, lax.rem(place - z + NZ, NZ)] = value[place * chunk : (place + 1) * chunk]

    def wgrad(a):
        chunks = a_buf[a].reshape(NZ * chunk, a_buf.shape[3])
        at[...] = jnp.maximum(chunks, jnp.zeros((), BF16)).T
        value = jnp.dot(at[...], stacked(a), preferred_element_type=F32).reshape(wacc.shape)
        if a == 0:
            wacc[...] = value
        else:
            wacc[...] += value

    def z1_first(d):
        z1(d, d).wait_recv()
        start(z2(d))
        for e in BOTH:
            start(y1(e, NEAR[1 - d], d))

    def z1_second(d):
        z1(d, 1 - d).wait_recv()
        for e in BOTH:
            start(y1(e, NEAR[1 - d], 1 - d))

    def z2_in(d):
        z2(d).wait_recv()
        for e in BOTH:
            start(y1(e, 2, d))

    def pass_y(d, b):
        y1(d, b, d).wait_recv()
        start(y2(d, b))

    def rest_y(d):
        for b in range(NZ):
            y1(d, b, 1 - d).wait_recv()

    def all_y2():
        for b in range(NZ):
            for d in BOTH:
                y2(d, b).wait_recv()

    def wcore_out():
        wb[...] = wacc[...].astype(BF16)
        for k in (0, 1):
            start(wcore(k))

    def wlo_out():
        for k in (0, 1):
            wcore(k).wait_recv()
        wz_out[...] = (wacc[2 * (1 - lo) + core] + wc_in[1 - lo].astype(F32)).astype(BF16)
        start(wlo())

    def wgrad_out():
        wlo().wait_recv()
        grad = wacc[tile] + wc_in[lo].astype(F32) + wz_in[...].astype(F32)
        for si in range(3):
            for ri in range(3):
                place = (si * 3 + ri) * width
                gk_ref[ri * 3 + si] = grad[:, place : place + width]

    steps = {
        "wcore": wcore_out,
        "wlo": wlo_out,
        "wfin": wgrad_out,
        "wgrad0": lambda: (own.wait(), wgrad(0)),
        "wgrad3": lambda: (rest_y(UP), wgrad(3)),
        "wgrad1": lambda: (rest_y(DOWN), wgrad(1)),
        "wgrad2": lambda: (all_y2(), wgrad(2)),
    }
    for a in range(NY):
        steps[f"dgrad{a}"] = functools.partial(dgrad, a)
    for d in BOTH:
        steps[f"z1a{d}"] = functools.partial(z1_first, d)
        steps[f"z1b{d}"] = functools.partial(z1_second, d)
        steps[f"z2_{d}"] = functools.partial(z2_in, d)
        for b in range(NZ):
            steps[f"pass{d}{b}"] = functools.partial(pass_y, d, b)
    for red in (red_y, red_z):
        for d in BOTH:
            for k in (0, 1):
                steps[f"{red.name}_far{k}{d}"] = functools.partial(red.send_far, d, k)
            steps[f"{red.name}_near2{d}"] = functools.partial(red.send_near2, d)
        for b in range(NZ):
            steps[f"{red.name}_dir{b}"] = functools.partial(red.send_direct, b)
            steps[f"{red.name}_dep{b}"] = functools.partial(red.send_relayed, b)
        steps[f"{red.name}_far2"] = red.send_far2
        steps[f"{red.name}_fin"] = red.finish
    assert set(ORDER) == set(steps) and len(ORDER) == len(steps)
    for n, name in enumerate(ORDER):
        with mark(f"{n:02}_{name}"):
            steps[name]()
    assert len(number.known) <= MESSAGES
    with mark("21_sends"):
        for copy in started:
            copy.wait_send()

        @pl.when(jnp.logical_not(first))
        def _():
            halo_down().wait_send()

        @pl.when(jnp.logical_not(last))
        def _():
            halo_up().wait_send()


def write_out(gi_ref, gk_ref, gi_out, gk_out, sem):
    copies = [
        pltpu.make_async_copy(gi_ref, gi_out, sem.at[0]),
        pltpu.make_async_copy(gk_ref, gk_out, sem.at[1]),
    ]
    for copy in copies:
        copy.start()
    for copy in copies:
        copy.wait()


def per_device(saved_input, upstream, weights):
    rows, cols, width = upstream.shape
    own_cols, channels = saved_input.shape[1], saved_input.shape[2]
    chunk = own_cols * rows
    x = jnp.transpose(saved_input, (1, 0, 2)).reshape(chunk, channels)
    hbm = pl.BlockSpec(memory_space=pl.ANY)
    vmem = pl.BlockSpec(memory_space=pltpu.VMEM)
    block = channels // 4
    y_rows = chunk - Z_ROWS
    gi_shape, gk_shape = (chunk, channels), (9, block, width)

    def landing(n):
        return [
            pltpu.VMEM((2, 2, n, channels), BF16),
            pltpu.VMEM((2, NZ, n, channels), BF16),
        ]

    def landing2(n):
        return [pltpu.VMEM((2, n // 2, channels), BF16), pltpu.VMEM((2, n, channels), BF16)]

    gi, gk = pl.pallas_call(
        kernel,
        name="conv_backward",
        out_shape=(pltpu.VMEM(gi_shape, BF16), pltpu.VMEM(gk_shape, F32)),
        in_specs=[hbm, hbm, hbm],
        out_specs=(vmem, vmem),
        scratch_shapes=[
            pltpu.VMEM((rows, cols, width), BF16),
            pltpu.VMEM((channels, 9 * width), BF16),
            pltpu.VMEM(((rows + 2) * cols, width), F32),
            pltpu.VMEM((cols + 2, rows, 9 * width), BF16),
            pltpu.VMEM((NY, NZ, chunk, channels), BF16),
            pltpu.VMEM((NY, NZ, chunk, channels), BF16),
            *landing(y_rows),
            *landing(Z_ROWS),
            *landing2(y_rows),
            *landing2(Z_ROWS),
            pltpu.VMEM((4, block, 9 * width), F32),
            pltpu.VMEM((channels, NZ * chunk), BF16),
            pltpu.VMEM((4, block, 9 * width), BF16),
            pltpu.VMEM((2, block, 9 * width), BF16),
            pltpu.VMEM((block, 9 * width), BF16),
            pltpu.VMEM((block, 9 * width), BF16),
            pltpu.VMEM((2, cols, width), BF16),
            pltpu.SemaphoreType.DMA((MESSAGES,)),
            pltpu.SemaphoreType.DMA((MESSAGES,)),
            pltpu.SemaphoreType.DMA((11,)),
        ],
        compiler_params=pltpu.CompilerParams(
            collective_id=0, has_side_effects=True, vmem_limit_bytes=56 * 1024 * 1024
        ),
    )(x, upstream, weights.reshape(9, channels, width))
    gi, gk = pl.pallas_call(
        write_out,
        name="write_out",
        out_shape=(jax.ShapeDtypeStruct(gi_shape, BF16), jax.ShapeDtypeStruct(gk_shape, F32)),
        in_specs=[vmem, vmem],
        out_specs=(hbm, hbm),
        scratch_shapes=[pltpu.SemaphoreType.DMA((2,))],
        compiler_params=pltpu.CompilerParams(vmem_limit_bytes=1024 * 1024),
    )(gi, gk)
    input_grad = jnp.transpose(gi.reshape(own_cols, rows, channels), (1, 0, 2))
    return input_grad, gk.reshape(3, 3, block, width)


def solution(mesh):
    placed = (P("tile", "filt", "chan"), P("tile", None, "filt"), P(None, None, "chan", "filt"))
    return jax.shard_map(
        per_device,
        mesh=mesh,
        in_specs=placed,
        out_specs=(P("tile", "filt", "chan"), P(None, None, ("chan", "tile"), "filt")),
        check_vma=False,
    )
```

```python
import functools
import math
from contextlib import nullcontext as mark

import jax
import jax.numpy as jnp
from jax import lax
from jax.experimental import pallas as pl
from jax.experimental.pallas import tpu as pltpu
from jax.sharding import PartitionSpec as P

BF16, F32 = jnp.bfloat16, jnp.float32
NY, NZ = 4, 4
UP, DOWN = 0, 1
BOTH = (UP, DOWN)
NEAR = (1, 3)
FAR_BLOCKS = ((2, 1), (3, 0))
RELAY = {2: (UP, 0), 1: (UP, 1), 3: (DOWN, 0), 0: (DOWN, 1)}
CLASSES = (("rz", "z", 64), ("ry", "y", 64), ("rw", "y", 64))
W_PARTS = 3
MESSAGES = 89

ORDER = (
    "pass00", "pass10", "dgrad2", "ry_far00", "z2_1", "z2_0", "rw_far00",
    "y1_011", "y1_130", "y1_030", "dgrad1", "y1_111", "dgrad0", "y1_031",
    "y1_110", "y1_010", "dgrad3", "ry_far01", "rz_far01", "y1_131", "y1_121",
    "rz_far00", "y1_020", "y1_120", "y1_021", "rz_far10", "rz_dir3", "pass03",
    "pass11", "rz_dir2", "rz_dir0", "rz_far11", "pass12", "pass01", "pass13",
    "pass02", "rz_dep2", "ry_dir2", "rz_dep3", "rz_dep0", "ry_dep2", "rw_dep2",
    "rz_dep1", "rz_dir1", "rw_far10", "rw_dir2", "rw_far01", "ry_far10", "wgrad0",
    "wgrad1", "wgrad3", "rw_dir1", "wgrad2_0", "wcore_0", "ry_far2", "ry_dir3",
    "rw_far11", "wgrad2_1", "ry_dep3", "ry_far11", "rw_far2", "wcore_1", "wlo_0",
    "rw_dep1", "wgrad2_2", "ry_dir1", "rw_dep3", "ry_dep1", "rw_dir3", "wlo_1",
    "ry_near21", "rz_far2", "rw_near20", "wfin_0", "rw_dir0", "ry_near20", "wcore_2",
    "rw_near21", "rz_near20", "rz_near21", "ry_dep0", "wlo_2", "ry_dir0", "rw_dep0",
    "rz_fin", "ry_fin", "wfin_1", "rw_fin", "wfin_2",
)


class Message:
    def __init__(self, make, key, landed):
        self.make, self.key, self.landed = make, key, landed

    def arrive(self):
        if self.key not in self.landed:
            self.landed.add(self.key)
            self.make().wait_recv()


def kernel(
    x_ref, u_ref, k_ref, gi_ref, gk_ref,
    u_vm, kc, uf, s_buf, a_buf, p_buf, wacc, at, wb, wc_in, wz_out, wz_in, halo, ssem, rsem, lsem, *landing,
):
    rows, cols, width = u_ref.shape
    chunk = x_ref.shape[0]
    half = chunk // 2
    own_cols = chunk // rows
    group_cols = NZ * own_cols
    taps = 3 * width
    filt, tile = lax.axis_index("filt"), lax.axis_index("tile")
    y, z = lax.div(filt, NZ), lax.rem(filt, NZ)
    lo, core = lax.div(tile, 2), lax.rem(tile, 2)
    numbers, landed, sent = {}, set(), []

    def zed(step):
        return lax.rem(z + step, NZ)

    def ycoord(step):
        return lax.rem(y + step, NY)

    def at_y(direction):
        return {"filt": ycoord(NEAR[direction]) * NZ + z}

    def at_z(direction):
        return {"filt": y * NZ + zed(NEAR[direction])}

    def message(key, src, dst, peer, send_sem=None):
        n = numbers.setdefault(key, len(numbers))

        def make():
            return pltpu.make_async_remote_copy(
                src_ref=src, dst_ref=dst, send_sem=ssem.at[0] if send_sem is None else send_sem,
                recv_sem=rsem.at[n], device_id=peer, device_id_type=pl.DeviceIdType.MESH,
            )

        return Message(make, key, landed)

    def start(move):
        copy = move.make()
        copy.start()
        sent.append(math.prod(copy.src_ref.shape) * 2)

    def arrive(move):
        move.arrive()

    other_core = {"tile": lo * 2 + 1 - core}
    other_lo = {"tile": (1 - lo) * 2 + core}
    cross = {"tile": (1 - lo) * 2 + 1 - core}

    barrier = pltpu.get_barrier_semaphore()
    peers = [at_y(UP), at_y(DOWN), at_z(UP), at_z(DOWN), other_core, other_lo, cross]
    for peer in peers:
        pl.semaphore_signal(barrier, inc=1, device_id=peer, device_id_type=pl.DeviceIdType.MESH)

    upstream_copy = pltpu.make_async_copy(u_ref, u_vm, lsem.at[10])
    upstream_copy.start()
    own = pltpu.make_async_copy(x_ref, a_buf.at[0, z], lsem.at[9])
    own.start()
    weights = []
    for si in range(3):
        for ri in range(3):
            place = si * 3 + ri
            copy = pltpu.make_async_copy(
                k_ref.at[ri * 3 + si], kc.at[:, pl.ds(place * width, width)], lsem.at[place]
            )
            copy.start()
            weights.append(copy)
    with mark("a_barrier"):
        pl.semaphore_wait(barrier, len(peers))

    def part(h):
        return pl.ds(h * half, half)

    def z1(d, h):
        return message(("z1", d, h), x_ref.at[part(h)], a_buf.at[0, z, part(h)], at_z(d))

    def z2(d):
        slot = a_buf.at[0, zed(NEAR[1 - d]), part(d)]
        return message(("z2", d), slot, slot, at_z(d))

    def y1(d, b, h):
        src = x_ref.at[part(h)] if b == 0 else a_buf.at[0, zed(b), part(h)]
        return message(("y1", d, b, h), src, a_buf.at[NEAR[1 - d], zed(b), part(h)], at_y(d))

    def y2(d, b):
        return message(
            ("y2", d, b), a_buf.at[NEAR[1 - d], zed(b), part(d)], a_buf.at[2, zed(b), part(d)], at_y(d)
        )

    def columns(p):
        return pl.ds(p * taps, taps)

    def wcore(k, p):
        src = wb.at[2 * k + 1 - core, :, columns(p)]
        return message(("wc", k, p), src, wc_in.at[k, :, columns(p)], other_core)

    def wlo(p):
        return message(("wz", p), wz_out.at[:, columns(p)], wz_in.at[:, columns(p)], other_lo)

    def halo_down():
        return message(("halo", 0), u_ref.at[0], halo.at[1], {"tile": tile - 1}, lsem.at[11]).make()

    def halo_up():
        return message(("halo", 1), u_ref.at[rows - 1], halo.at[0], {"tile": tile + 1}, lsem.at[12]).make()

    class Reduce:
        def __init__(self, name, ring, low, count, bufs):
            self.name, self.low, self.count = name, low, count
            self.swap = ring == "z"
            self.first, self.second = (at_z, at_y) if self.swap else (at_y, at_z)
            self.far_in, self.near_in, self.far2_in, self.near2_in = bufs

        def block(self, i, j, h=None):
            low, count = self.low, self.count
            if h is not None:
                count //= 2
                low += h * count
            slot = (j, i) if self.swap else (i, j)
            return (*slot, pl.ds(low, count))

        def far(self, d, k):
            src = p_buf.at[self.block(2, FAR_BLOCKS[d][k])]
            return message((self.name, "far", d, k), src, self.far_in.at[d, k], self.first(d))

        def near(self, d, b):
            src = p_buf.at[self.block(NEAR[d], b)]
            return message((self.name, "near", d, b), src, self.near_in.at[d, b], self.first(d))

        def far2(self, d):
            src = p_buf.at[self.block(0, 2, d)]
            return message((self.name, "far2", d), src, self.far2_in.at[d], self.second(d))

        def near2(self, d):
            src = p_buf.at[self.block(0, NEAR[d])]
            return message((self.name, "near2", d), src, self.near2_in.at[d], self.second(d))

        def send_far(self, d, k):
            start(self.far(d, k))

        def send_direct(self, b):
            start(self.near(1 - RELAY[b][0], b))

        def send_relayed(self, b):
            d, k = RELAY[b]
            arrive(self.far(d, k))
            slot = self.block(NEAR[d], b)
            p_buf[slot] = (p_buf[slot].astype(F32) + self.far_in[d, k].astype(F32)).astype(BF16)
            start(self.near(d, b))

        def near_sum(self, b):
            for d in BOTH:
                arrive(self.near(d, b))
            own_term = p_buf[self.block(0, b)].astype(F32)
            return own_term + self.near_in[UP, b].astype(F32) + self.near_in[DOWN, b].astype(F32)

        def send_far2(self):
            p_buf[self.block(0, 2)] = self.near_sum(2).astype(BF16)
            for d in BOTH:
                start(self.far2(d))

        def send_near2(self, d):
            b, n = NEAR[d], self.count // 2
            total = self.near_sum(b)
            arrive(self.far2(d))
            p_buf[self.block(0, b, 1 - d)] = total[(1 - d) * n : (2 - d) * n].astype(BF16)
            p_buf[self.block(0, b, d)] = (
                total[d * n : (d + 1) * n] + self.far2_in[d].astype(F32)
            ).astype(BF16)
            start(self.near2(d))

        def finish(self):
            total = self.near_sum(0)
            for d in BOTH:
                arrive(self.near2(d))
            total += self.near2_in[UP].astype(F32) + self.near2_in[DOWN].astype(F32)
            place = pl.ds(self.low, self.count)
            gi_ref[place] = jnp.where(a_buf[0, z, place] > 0, total, 0.0).astype(BF16)

    first, last = tile == 0, tile == 3

    @pl.when(jnp.logical_not(first))
    def _():
        halo_down().start()

    @pl.when(jnp.logical_not(last))
    def _():
        halo_up().start()

    for h in BOTH:
        for d in BOTH:
            start(z1(d, h ^ d))
            start(y1(d, 0, h ^ d))

    with mark("b_uf"):
        upstream_copy.wait()

        @pl.loop(0, rows)
        def _(i):
            uf[pl.ds(pl.multiple_of((i + 1) * cols, 8), cols), :] = u_vm[i].astype(F32)

    s_buf[1, :, 2 * taps :] = jnp.zeros((rows, taps), BF16)
    s_buf[cols, :, :taps] = jnp.zeros((rows, taps), BF16)
    bottom = (rows + 1) * cols
    with mark("c_halo"):

        @pl.when(first)
        def _():
            uf[:cols, :] = jnp.zeros((cols, width), F32)

        @pl.when(jnp.logical_not(first))
        def _():
            halo_up().wait_recv()
            uf[:cols, :] = halo[0].astype(F32)

        @pl.when(last)
        def _():
            uf[bottom:, :] = jnp.zeros((cols, width), F32)

        @pl.when(jnp.logical_not(last))
        def _():
            halo_down().wait_recv()
            uf[bottom:, :] = halo[1].astype(F32)

    with mark("d_im2col"):

        @pl.loop(0, cols)
        def _(j):
            for ri in range(3):
                value = uf[pl.ds((2 - ri) * cols + j, rows, stride=cols), :].astype(BF16)
                for si in range(3):
                    s_buf[j + si, :, pl.ds(si * taps + ri * width, width)] = value

        for copy in weights:
            copy.wait()

    def stacked(a, lanes=slice(None)):
        block = s_buf[pl.ds(ycoord(a) * group_cols + 1, group_cols), :, lanes]
        return block.reshape(NZ * chunk, block.shape[2])

    def dgrad(a):
        value = lax.dot_general(
            stacked(a), kc[...], (((1,), (1,)), ((), ())), preferred_element_type=F32
        ).astype(BF16)
        for place in range(NZ):
            p_buf[a, lax.rem(place - z + NZ, NZ)] = value[place * chunk : (place + 1) * chunk]

    def activate(a):
        chunks = a_buf[a].reshape(NZ * chunk, a_buf.shape[3])
        at[...] = jnp.maximum(chunks, jnp.zeros((), BF16)).T

    def wgrad(a):
        activate(a)
        value = jnp.dot(at[...], stacked(a), preferred_element_type=F32).reshape(wacc.shape)
        if a == 0:
            wacc[...] = value
        else:
            wacc[...] += value

    def wgrad_z():
        own.wait()
        for d in BOTH:
            for h in BOTH:
                arrive(z1(d, h))
            arrive(z2(d))
        wgrad(0)

    def wgrad_y(d):
        for b in range(NZ):
            for h in BOTH:
                arrive(y1(d, b, h))
        wgrad(NEAR[1 - d])

    def wgrad_last(p):
        if p == 0:
            for b in range(NZ):
                for d in BOTH:
                    arrive(y2(d, b))
            activate(2)
        value = jnp.dot(at[...], stacked(2, columns(p)), preferred_element_type=F32)
        wacc[:, :, columns(p)] += value.reshape(wacc.shape[0], wacc.shape[1], taps)

    def wcore_out(p):
        wb[:, :, columns(p)] = wacc[:, :, columns(p)].astype(BF16)
        for k in (0, 1):
            start(wcore(k, p))

    def wlo_out(p):
        for k in (0, 1):
            arrive(wcore(k, p))
        total = wacc[2 * (1 - lo) + core, :, columns(p)] + wc_in[1 - lo, :, columns(p)].astype(F32)
        wz_out[:, columns(p)] = total.astype(BF16)
        start(wlo(p))

    def wgrad_out(p):
        arrive(wlo(p))
        grad = wacc[tile, :, columns(p)] + wc_in[lo, :, columns(p)].astype(F32)
        grad += wz_in[:, columns(p)].astype(F32)
        for ri in range(3):
            gk_ref[ri * 3 + p] = grad[:, ri * width : (ri + 1) * width]

    def pass_z(d):
        arrive(z1(d, d))
        start(z2(d))

    def pass_to_y(e, b, h):
        arrive(z2(h) if b == 2 else z1(UP if b == 3 else DOWN, h))
        start(y1(e, b, h))

    def pass_y(d, b):
        arrive(y1(d, b, d))
        start(y2(d, b))

    steps = {
        "wgrad0": wgrad_z,
        "wgrad3": functools.partial(wgrad_y, UP),
        "wgrad1": functools.partial(wgrad_y, DOWN),
    }
    for a in range(NY):
        steps[f"dgrad{a}"] = functools.partial(dgrad, a)
    for d in BOTH:
        steps[f"z2_{d}"] = functools.partial(pass_z, d)
        for b in range(NZ):
            steps[f"pass{d}{b}"] = functools.partial(pass_y, d, b)
        for b in (1, 2, 3):
            for h in BOTH:
                steps[f"y1_{d}{b}{h}"] = functools.partial(pass_to_y, d, b, h)
    for p in range(W_PARTS):
        steps[f"wgrad2_{p}"] = functools.partial(wgrad_last, p)
        steps[f"wcore_{p}"] = functools.partial(wcore_out, p)
        steps[f"wlo_{p}"] = functools.partial(wlo_out, p)
        steps[f"wfin_{p}"] = functools.partial(wgrad_out, p)
    low = 0
    for n, (name, ring, count) in enumerate(CLASSES):
        red = Reduce(name, ring, low, count, landing[4 * n : 4 * n + 4])
        low += count
        for d in BOTH:
            for k in (0, 1):
                steps[f"{name}_far{k}{d}"] = functools.partial(red.send_far, d, k)
            steps[f"{name}_near2{d}"] = functools.partial(red.send_near2, d)
        for b in range(NZ):
            steps[f"{name}_dir{b}"] = functools.partial(red.send_direct, b)
            steps[f"{name}_dep{b}"] = functools.partial(red.send_relayed, b)
        steps[f"{name}_far2"] = red.send_far2
        steps[f"{name}_fin"] = red.finish
    assert set(ORDER) == set(steps) and len(ORDER) == len(steps)
    for n, name in enumerate(ORDER):
        with mark(f"{n:03}_{name}"):
            steps[name]()
    assert len(numbers) == MESSAGES
    with mark("y_sends"):
        column = rows * 9 * width * 2
        assert sum(sent) % column == 0
        everything = s_buf.at[pl.ds(0, sum(sent) // column)]
        pltpu.make_async_copy(everything, everything, ssem.at[0]).wait()

        @pl.when(jnp.logical_not(first))
        def _():
            halo_down().wait_send()

        @pl.when(jnp.logical_not(last))
        def _():
            halo_up().wait_send()


def write_out(gi_ref, gk_ref, gi_out, gk_out, sem):
    copies = [
        pltpu.make_async_copy(gi_ref, gi_out, sem.at[0]),
        pltpu.make_async_copy(gk_ref, gk_out, sem.at[1]),
    ]
    for copy in copies:
        copy.start()
    for copy in copies:
        copy.wait()


def per_device(saved_input, upstream, weights):
    rows, cols, width = upstream.shape
    own_cols, channels = saved_input.shape[1], saved_input.shape[2]
    chunk = own_cols * rows
    x = jnp.transpose(saved_input, (1, 0, 2)).reshape(chunk, channels)
    hbm = pl.BlockSpec(memory_space=pl.ANY)
    vmem = pl.BlockSpec(memory_space=pltpu.VMEM)
    block = channels // 4
    gi_shape, gk_shape = (chunk, channels), (9, block, width)
    landing = []
    for _, _, n in CLASSES:
        for shape in ((2, 2, n), (2, NZ, n), (2, n // 2), (2, n)):
            landing.append(pltpu.VMEM((*shape, channels), BF16))
    gi, gk = pl.pallas_call(
        kernel,
        name="conv_backward",
        out_shape=(pltpu.VMEM(gi_shape, BF16), pltpu.VMEM(gk_shape, F32)),
        in_specs=[hbm, hbm, hbm],
        out_specs=(vmem, vmem),
        scratch_shapes=[
            pltpu.VMEM((rows, cols, width), BF16),
            pltpu.VMEM((channels, 9 * width), BF16),
            pltpu.VMEM(((rows + 2) * cols, width), F32),
            pltpu.VMEM((cols + 2, rows, 9 * width), BF16),
            pltpu.VMEM((NY, NZ, chunk, channels), BF16),
            pltpu.VMEM((NY, NZ, chunk, channels), BF16),
            pltpu.VMEM((4, block, 9 * width), F32),
            pltpu.VMEM((channels, NZ * chunk), BF16),
            pltpu.VMEM((4, block, 9 * width), BF16),
            pltpu.VMEM((2, block, 9 * width), BF16),
            pltpu.VMEM((block, 9 * width), BF16),
            pltpu.VMEM((block, 9 * width), BF16),
            pltpu.VMEM((2, cols, width), BF16),
            pltpu.SemaphoreType.DMA((1,)),
            pltpu.SemaphoreType.DMA((MESSAGES,)),
            pltpu.SemaphoreType.DMA((13,)),
            *landing,
        ],
        compiler_params=pltpu.CompilerParams(
            collective_id=0, has_side_effects=True, vmem_limit_bytes=56 * 1024 * 1024
        ),
    )(x, upstream, weights.reshape(9, channels, width))
    gi, gk = pl.pallas_call(
        write_out,
        name="write_out",
        out_shape=(jax.ShapeDtypeStruct(gi_shape, BF16), jax.ShapeDtypeStruct(gk_shape, F32)),
        in_specs=[vmem, vmem],
        out_specs=(hbm, hbm),
        scratch_shapes=[pltpu.SemaphoreType.DMA((2,))],
        compiler_params=pltpu.CompilerParams(vmem_limit_bytes=1024 * 1024),
    )(gi, gk)
    input_grad = jnp.transpose(gi.reshape(own_cols, rows, channels), (1, 0, 2))
    return input_grad, gk.reshape(3, 3, block, width)


def solution(mesh):
    placed = (P("tile", "filt", "chan"), P("tile", None, "filt"), P(None, None, "chan", "filt"))
    return jax.shard_map(
        per_device,
        mesh=mesh,
        in_specs=placed,
        out_specs=(P("tile", "filt", "chan"), P(None, None, ("chan", "tile"), "filt")),
        check_vma=False,
    )
```

```python
import functools
import math
from contextlib import nullcontext as mark

import jax
import jax.numpy as jnp
from jax import lax
from jax.experimental import pallas as pl
from jax.experimental.pallas import tpu as pltpu
from jax.sharding import PartitionSpec as P

BF16, F32 = jnp.bfloat16, jnp.float32
NY, NZ = 4, 4
UP, DOWN = 0, 1
BOTH = (UP, DOWN)
NEAR = (1, 3)
FAR_BLOCKS = ((2, 1), (3, 0))
RELAY = {2: (UP, 0), 1: (UP, 1), 3: (DOWN, 0), 0: (DOWN, 1)}
CLASSES = (("rz", "z", 64), ("ry", "y", 64), ("rw", "y", 64))
W_PARTS = 3
MESSAGES = 58

ORDER = (
    8, 19, 5, 57, 7, 24, 13, 18, 6, 27, 16, 4, 3, 42, 45, 12, 41, 28, 23, 17, 14, 15, 26, 11,
    20, 44, 25, 9, 47, 50, 49, 22, 51, 21, 0, 67, 48, 52, 10, 60, 1, 76, 68, 73, 58, 54, 74, 65,
    2, 53, 29, 30, 81, 83, 71, 33, 70, 34, 61, 84, 31, 69, 66, 85, 55, 35, 82, 37, 38, 87, 86, 79,
    39, 32, 77, 59, 62, 63, 78, 64, 43, 46, 36, 75, 80, 56, 72, 40, 88,
)


class Message:
    def __init__(self, make, key, landed):
        self.make, self.key, self.landed = make, key, landed

    def arrive(self):
        if self.key not in self.landed:
            self.landed.add(self.key)
            self.make().wait_recv()


def kernel(
    x_ref, u_ref, k_ref, gi_ref, gk_ref,
    u_vm, kc, uf, s_buf, a_buf, p_buf, wacc, at, wb, wc_in, wz_out, wz_in, halo, ssem, rsem, lsem, *landing,
):
    rows, cols, width = u_ref.shape
    chunk = x_ref.shape[0]
    half = chunk // 2
    own_cols = chunk // rows
    group_cols = NZ * own_cols
    taps = 3 * width
    filt, tile = lax.axis_index("filt"), lax.axis_index("tile")
    y, z = lax.div(filt, NZ), lax.rem(filt, NZ)
    lo, core = lax.div(tile, 2), lax.rem(tile, 2)
    numbers, landed, sent = {}, set(), []

    def zed(step):
        return lax.rem(z + step, NZ)

    def ycoord(step):
        return lax.rem(y + step, NY)

    def at_y(direction):
        return {"filt": ycoord(NEAR[direction]) * NZ + z}

    def at_z(direction):
        return {"filt": y * NZ + zed(NEAR[direction])}

    def message(key, src, dst, peer, send_sem=None, group=None):
        n = numbers.setdefault(group or key, len(numbers))

        def make():
            return pltpu.make_async_remote_copy(
                src_ref=src, dst_ref=dst, send_sem=ssem.at[0] if send_sem is None else send_sem,
                recv_sem=rsem.at[n], device_id=peer, device_id_type=pl.DeviceIdType.MESH,
            )

        return Message(make, key, landed)

    def start(move):
        copy = move.make()
        copy.start()
        sent.append(math.prod(copy.src_ref.shape) * 2)

    def arrive(move):
        move.arrive()

    def arrive_all(group, place):
        if group not in landed:
            landed.add(group)
            pltpu.make_async_copy(place, place, rsem.at[numbers[group]]).wait()

    other_core = {"tile": lo * 2 + 1 - core}
    other_lo = {"tile": (1 - lo) * 2 + core}
    cross = {"tile": (1 - lo) * 2 + 1 - core}

    barrier = pltpu.get_barrier_semaphore()
    peers = [at_y(UP), at_y(DOWN), at_z(UP), at_z(DOWN), other_core, other_lo, cross]
    for peer in peers:
        pl.semaphore_signal(barrier, inc=1, device_id=peer, device_id_type=pl.DeviceIdType.MESH)

    upstream_copy = pltpu.make_async_copy(u_ref, u_vm, lsem.at[1])
    upstream_copy.start()
    own = pltpu.make_async_copy(x_ref, a_buf.at[0, z], lsem.at[2])
    own.start()
    for si in range(3):
        for ri in range(3):
            place = kc.at[:, pl.ds((si * 3 + ri) * width, width)]
            pltpu.make_async_copy(k_ref.at[ri * 3 + si], place, lsem.at[0]).start()
    with mark("a_barrier"):
        pl.semaphore_wait(barrier, len(peers))

    def part(h):
        return pl.ds(h * half, half)

    def z1(d, h):
        return message(("z1", d, h), x_ref.at[part(h)], a_buf.at[0, z, part(h)], at_z(d))

    def z2(d):
        slot = a_buf.at[0, zed(NEAR[1 - d]), part(d)]
        return message(("z2", d), slot, slot, at_z(d))

    def y1(d, b, h):
        src = x_ref.at[part(h)] if b == 0 else a_buf.at[0, zed(b), part(h)]
        place = a_buf.at[NEAR[1 - d], zed(b), part(h)]
        return message(("y1", d, b, h), src, place, at_y(d), group=None if h == d else ("y1", d))

    def y2(d, b):
        src, place = a_buf.at[NEAR[1 - d], zed(b), part(d)], a_buf.at[2, zed(b), part(d)]
        return message(("y2", d, b), src, place, at_y(d), group=("y2",))

    def columns(p):
        return pl.ds(p * taps, taps)

    def wcore(k, p):
        src = wb.at[2 * k + 1 - core, :, columns(p)]
        return message(("wc", k, p), src, wc_in.at[k, :, columns(p)], other_core, group=("wc", p))

    def wlo(p):
        return message(("wz", p), wz_out.at[:, columns(p)], wz_in.at[:, columns(p)], other_lo)

    def halo_down():
        return message(("halo", 0), u_ref.at[0], halo.at[1], {"tile": tile - 1}, lsem.at[3]).make()

    def halo_up():
        return message(("halo", 1), u_ref.at[rows - 1], halo.at[0], {"tile": tile + 1}, lsem.at[4]).make()

    class Reduce:
        def __init__(self, name, ring, low, count, bufs):
            self.name, self.low, self.count = name, low, count
            self.swap = ring == "z"
            self.first, self.second = (at_z, at_y) if self.swap else (at_y, at_z)
            self.far_in, self.near_in, self.far2_in, self.near2_in = bufs

        def block(self, i, j, h=None):
            low, count = self.low, self.count
            if h is not None:
                count //= 2
                low += h * count
            slot = (j, i) if self.swap else (i, j)
            return (*slot, pl.ds(low, count))

        def far(self, d, k):
            src = p_buf.at[self.block(2, FAR_BLOCKS[d][k])]
            return message((self.name, "far", d, k), src, self.far_in.at[d, k], self.first(d))

        def near(self, d, b):
            src = p_buf.at[self.block(NEAR[d], b)]
            place, group = self.near_in.at[d, b], (self.name, "near", b)
            return message((self.name, "near", d, b), src, place, self.first(d), group=group)

        def far2(self, d):
            src = p_buf.at[self.block(0, 2, d)]
            return message((self.name, "far2", d), src, self.far2_in.at[d], self.second(d))

        def near2(self, d):
            src = p_buf.at[self.block(0, NEAR[d])]
            place, group = self.near2_in.at[d], (self.name, "near2")
            return message((self.name, "near2", d), src, place, self.second(d), group=group)

        def send_far(self, d, k):
            start(self.far(d, k))

        def send_direct(self, b):
            start(self.near(1 - RELAY[b][0], b))

        def send_relayed(self, b):
            d, k = RELAY[b]
            arrive(self.far(d, k))
            slot = self.block(NEAR[d], b)
            p_buf[slot] = (p_buf[slot].astype(F32) + self.far_in[d, k].astype(F32)).astype(BF16)
            start(self.near(d, b))

        def near_sum(self, b):
            arrive_all((self.name, "near", b), self.near_in.at[:, b])
            own_term = p_buf[self.block(0, b)].astype(F32)
            return own_term + self.near_in[UP, b].astype(F32) + self.near_in[DOWN, b].astype(F32)

        def send_far2(self):
            p_buf[self.block(0, 2)] = self.near_sum(2).astype(BF16)
            for d in BOTH:
                start(self.far2(d))

        def send_near2(self, d):
            b, n = NEAR[d], self.count // 2
            total = self.near_sum(b)
            arrive(self.far2(d))
            p_buf[self.block(0, b, 1 - d)] = total[(1 - d) * n : (2 - d) * n].astype(BF16)
            p_buf[self.block(0, b, d)] = (
                total[d * n : (d + 1) * n] + self.far2_in[d].astype(F32)
            ).astype(BF16)
            start(self.near2(d))

        def finish(self):
            total = self.near_sum(0)
            arrive_all((self.name, "near2"), self.near2_in)
            total += self.near2_in[UP].astype(F32) + self.near2_in[DOWN].astype(F32)
            place = pl.ds(self.low, self.count)
            gi_ref[place] = jnp.where(a_buf[0, z, place] > 0, total, 0.0).astype(BF16)

    first, last = tile == 0, tile == 3

    @pl.when(jnp.logical_not(first))
    def _():
        halo_down().start()

    @pl.when(jnp.logical_not(last))
    def _():
        halo_up().start()

    for h in BOTH:
        for d in BOTH:
            start(z1(d, h ^ d))
            start(y1(d, 0, h ^ d))

    with mark("b_uf"):
        upstream_copy.wait()

        @pl.loop(0, rows)
        def _(i):
            uf[pl.ds(pl.multiple_of((i + 1) * cols, 8), cols), :] = u_vm[i].astype(F32)

    s_buf[1, :, 2 * taps :] = jnp.zeros((rows, taps), BF16)
    s_buf[cols, :, :taps] = jnp.zeros((rows, taps), BF16)
    bottom = (rows + 1) * cols
    with mark("c_halo"):

        @pl.when(first)
        def _():
            uf[:cols, :] = jnp.zeros((cols, width), F32)

        @pl.when(jnp.logical_not(first))
        def _():
            halo_up().wait_recv()
            uf[:cols, :] = halo[0].astype(F32)

        @pl.when(last)
        def _():
            uf[bottom:, :] = jnp.zeros((cols, width), F32)

        @pl.when(jnp.logical_not(last))
        def _():
            halo_down().wait_recv()
            uf[bottom:, :] = halo[1].astype(F32)

    with mark("d_im2col"):

        @pl.loop(0, cols)
        def _(j):
            for ri in range(3):
                value = uf[pl.ds((2 - ri) * cols + j, rows, stride=cols), :].astype(BF16)
                for si in range(3):
                    s_buf[j + si, :, pl.ds(si * taps + ri * width, width)] = value

        pltpu.make_async_copy(kc, kc, lsem.at[0]).wait()

    def stacked(a, lanes=slice(None)):
        block = s_buf[pl.ds(ycoord(a) * group_cols + 1, group_cols), :, lanes]
        return block.reshape(NZ * chunk, block.shape[2])

    def dgrad(a):
        value = lax.dot_general(
            stacked(a), kc[...], (((1,), (1,)), ((), ())), preferred_element_type=F32
        ).astype(BF16)
        for place in range(NZ):
            p_buf[a, lax.rem(place - z + NZ, NZ)] = value[place * chunk : (place + 1) * chunk]

    def activate(a):
        chunks = a_buf[a].reshape(NZ * chunk, a_buf.shape[3])
        at[...] = jnp.maximum(chunks, jnp.zeros((), BF16)).T

    def wgrad(a):
        activate(a)
        value = jnp.dot(at[...], stacked(a), preferred_element_type=F32).reshape(wacc.shape)
        if a == 0:
            wacc[...] = value
        else:
            wacc[...] += value

    def wgrad_z():
        own.wait()
        for d in BOTH:
            for h in BOTH:
                arrive(z1(d, h))
            arrive(z2(d))
        wgrad(0)

    def wgrad_y(d):
        for b in range(NZ):
            arrive(y1(d, b, d))
        arrive_all(("y1", d), a_buf.at[NEAR[1 - d], :, part(1 - d)])
        wgrad(NEAR[1 - d])

    def wgrad_last(p):
        if p == 0:
            arrive_all(("y2",), a_buf.at[2])
            activate(2)
        value = jnp.dot(at[...], stacked(2, columns(p)), preferred_element_type=F32)
        wacc[:, :, columns(p)] += value.reshape(wacc.shape[0], wacc.shape[1], taps)

    def wcore_out(p):
        wb[:, :, columns(p)] = wacc[:, :, columns(p)].astype(BF16)
        for k in (0, 1):
            start(wcore(k, p))

    def wlo_out(p):
        arrive_all(("wc", p), wc_in.at[:, :, columns(p)])
        total = wacc[2 * (1 - lo) + core, :, columns(p)] + wc_in[1 - lo, :, columns(p)].astype(F32)
        wz_out[:, columns(p)] = total.astype(BF16)
        start(wlo(p))

    def wgrad_out(p):
        arrive(wlo(p))
        grad = wacc[tile, :, columns(p)] + wc_in[lo, :, columns(p)].astype(F32)
        grad += wz_in[:, columns(p)].astype(F32)
        for ri in range(3):
            gk_ref[ri * 3 + p] = grad[:, ri * width : (ri + 1) * width]

    def pass_z(d):
        arrive(z1(d, d))
        start(z2(d))

    def pass_to_y(e, b, h):
        arrive(z2(h) if b == 2 else z1(UP if b == 3 else DOWN, h))
        start(y1(e, b, h))

    def pass_y(d, b):
        arrive(y1(d, b, d))
        start(y2(d, b))

    steps = {
        "wgrad0": wgrad_z,
        "wgrad3": functools.partial(wgrad_y, UP),
        "wgrad1": functools.partial(wgrad_y, DOWN),
    }
    for a in range(NY):
        steps[f"dgrad{a}"] = functools.partial(dgrad, a)
    for d in BOTH:
        steps[f"z2_{d}"] = functools.partial(pass_z, d)
        for b in range(NZ):
            steps[f"pass{d}{b}"] = functools.partial(pass_y, d, b)
        for b in (1, 2, 3):
            for h in BOTH:
                steps[f"y1_{d}{b}{h}"] = functools.partial(pass_to_y, d, b, h)
    for p in range(W_PARTS):
        steps[f"wgrad2_{p}"] = functools.partial(wgrad_last, p)
        steps[f"wcore_{p}"] = functools.partial(wcore_out, p)
        steps[f"wlo_{p}"] = functools.partial(wlo_out, p)
        steps[f"wfin_{p}"] = functools.partial(wgrad_out, p)
    low = 0
    for n, (name, ring, count) in enumerate(CLASSES):
        red = Reduce(name, ring, low, count, landing[4 * n : 4 * n + 4])
        low += count
        for d in BOTH:
            for k in (0, 1):
                steps[f"{name}_far{k}{d}"] = functools.partial(red.send_far, d, k)
            steps[f"{name}_near2{d}"] = functools.partial(red.send_near2, d)
        for b in range(NZ):
            steps[f"{name}_dir{b}"] = functools.partial(red.send_direct, b)
            steps[f"{name}_dep{b}"] = functools.partial(red.send_relayed, b)
        steps[f"{name}_far2"] = red.send_far2
        steps[f"{name}_fin"] = red.finish
    listed = list(steps.items())
    assert sorted(ORDER) == list(range(len(listed)))
    for n, place in enumerate(ORDER):
        name, step = listed[place]
        with mark(f"{n:03}_{name}"):
            step()
    assert len(numbers) == MESSAGES
    with mark("y_sends"):
        column = rows * 9 * width * 2
        assert sum(sent) % column == 0
        everything = s_buf.at[pl.ds(0, sum(sent) // column)]
        pltpu.make_async_copy(everything, everything, ssem.at[0]).wait()

        @pl.when(jnp.logical_not(first))
        def _():
            halo_down().wait_send()

        @pl.when(jnp.logical_not(last))
        def _():
            halo_up().wait_send()


def write_out(gi_ref, gk_ref, gi_out, gk_out, sem):
    copies = [
        pltpu.make_async_copy(gi_ref, gi_out, sem.at[0]),
        pltpu.make_async_copy(gk_ref, gk_out, sem.at[1]),
    ]
    for copy in copies:
        copy.start()
    for copy in copies:
        copy.wait()


def per_device(saved_input, upstream, weights):
    rows, cols, width = upstream.shape
    own_cols, channels = saved_input.shape[1], saved_input.shape[2]
    chunk = own_cols * rows
    x = jnp.transpose(saved_input, (1, 0, 2)).reshape(chunk, channels)
    hbm = pl.BlockSpec(memory_space=pl.ANY)
    vmem = pl.BlockSpec(memory_space=pltpu.VMEM)
    block = channels // 4
    gi_shape, gk_shape = (chunk, channels), (9, block, width)
    landing = []
    for _, _, n in CLASSES:
        for shape in ((2, 2, n), (2, NZ, n), (2, n // 2), (2, n)):
            landing.append(pltpu.VMEM((*shape, channels), BF16))
    gi, gk = pl.pallas_call(
        kernel,
        name="conv_backward",
        out_shape=(pltpu.VMEM(gi_shape, BF16), pltpu.VMEM(gk_shape, F32)),
        in_specs=[hbm, hbm, hbm],
        out_specs=(vmem, vmem),
        scratch_shapes=[
            pltpu.VMEM((rows, cols, width), BF16),
            pltpu.VMEM((channels, 9 * width), BF16),
            pltpu.VMEM(((rows + 2) * cols, width), F32),
            pltpu.VMEM((cols + 2, rows, 9 * width), BF16),
            pltpu.VMEM((NY, NZ, chunk, channels), BF16),
            pltpu.VMEM((NY, NZ, chunk, channels), BF16),
            pltpu.VMEM((4, block, 9 * width), F32),
            pltpu.VMEM((channels, NZ * chunk), BF16),
            pltpu.VMEM((4, block, 9 * width), BF16),
            pltpu.VMEM((2, block, 9 * width), BF16),
            pltpu.VMEM((block, 9 * width), BF16),
            pltpu.VMEM((block, 9 * width), BF16),
            pltpu.VMEM((2, cols, width), BF16),
            pltpu.SemaphoreType.DMA((1,)),
            pltpu.SemaphoreType.DMA((MESSAGES,)),
            pltpu.SemaphoreType.DMA((5,)),
            *landing,
        ],
        compiler_params=pltpu.CompilerParams(
            collective_id=0, has_side_effects=True, vmem_limit_bytes=56 * 1024 * 1024
        ),
    )(x, upstream, weights.reshape(9, channels, width))
    gi, gk = pl.pallas_call(
        write_out,
        name="write_out",
        out_shape=(jax.ShapeDtypeStruct(gi_shape, BF16), jax.ShapeDtypeStruct(gk_shape, F32)),
        in_specs=[vmem, vmem],
        out_specs=(hbm, hbm),
        scratch_shapes=[pltpu.SemaphoreType.DMA((2,))],
        compiler_params=pltpu.CompilerParams(vmem_limit_bytes=1024 * 1024),
    )(gi, gk)
    input_grad = jnp.transpose(gi.reshape(own_cols, rows, channels), (1, 0, 2))
    return input_grad, gk.reshape(3, 3, block, width)


def solution(mesh):
    placed = (P("tile", "filt", "chan"), P("tile", None, "filt"), P(None, None, "chan", "filt"))
    return jax.shard_map(
        per_device,
        mesh=mesh,
        in_specs=placed,
        out_specs=(P("tile", "filt", "chan"), P(None, None, ("chan", "tile"), "filt")),
        check_vma=False,
    )
```

```python
import functools
import math
from contextlib import nullcontext as mark

import jax
import jax.numpy as jnp
from jax import lax
from jax.experimental import pallas as pl
from jax.experimental.pallas import tpu as pltpu
from jax.sharding import PartitionSpec as P

BF16, F32 = jnp.bfloat16, jnp.float32
NY, NZ = 4, 4
UP, DOWN = 0, 1
BOTH = (UP, DOWN)
NEAR = (1, 3)
FAR_BLOCKS = ((2, 1), (3, 0))
RELAY = {2: (UP, 0), 1: (UP, 1), 3: (DOWN, 0), 0: (DOWN, 1)}
CLASSES = (("rz", "z", 64), ("ry", "y", 64), ("rw", "y", 64))
W_PARTS = 3
MESSAGES = 58

ORDER = (
    8, 19, 5, 57, 7, 24, 13, 18, 6, 27, 16, 4, 3, 42, 45, 12, 41, 28, 23, 17, 14, 15, 26, 11,
    20, 44, 25, 9, 47, 50, 49, 22, 51, 21, 0, 67, 48, 52, 10, 60, 1, 76, 68, 73, 58, 54, 74, 65,
    2, 53, 29, 30, 81, 83, 71, 33, 70, 34, 61, 84, 31, 69, 66, 85, 55, 35, 82, 37, 38, 87, 86, 79,
    39, 32, 77, 59, 62, 63, 78, 64, 43, 46, 36, 75, 80, 56, 72, 40, 88,
)


class Message:
    def __init__(self, make, key, landed):
        self.make, self.key, self.landed = make, key, landed

    def arrive(self):
        if self.key not in self.landed:
            self.landed.add(self.key)
            self.make().wait_recv()


def kernel(
    x_ref, u_ref, k_ref, gi_ref, gk_ref,
    u_vm, kc, uf, s_buf, a_buf, p_buf, wacc, at, wb, wc_in, wz_out, wz_in, halo, ssem, rsem, lsem, *landing,
):
    rows, cols, width = u_ref.shape
    chunk = x_ref.shape[0]
    half = chunk // 2
    own_cols = chunk // rows
    group_cols = NZ * own_cols
    taps = 3 * width
    filt, tile = lax.axis_index("filt"), lax.axis_index("tile")
    y, z = lax.div(filt, NZ), lax.rem(filt, NZ)
    lo, core = lax.div(tile, 2), lax.rem(tile, 2)
    numbers, landed, sent = {}, set(), []

    def zed(step):
        return lax.rem(z + step, NZ)

    def ycoord(step):
        return lax.rem(y + step, NY)

    def at_y(direction):
        return {"filt": ycoord(NEAR[direction]) * NZ + z}

    def at_z(direction):
        return {"filt": y * NZ + zed(NEAR[direction])}

    def message(key, src, dst, peer, send_sem=None, group=None):
        n = numbers.setdefault(group or key, len(numbers))

        def make():
            return pltpu.make_async_remote_copy(
                src_ref=src, dst_ref=dst, send_sem=ssem.at[0] if send_sem is None else send_sem,
                recv_sem=rsem.at[n], device_id=peer, device_id_type=pl.DeviceIdType.MESH,
            )

        return Message(make, key, landed)

    def start(move):
        copy = move.make()
        copy.start()
        sent.append(math.prod(copy.src_ref.shape) * 2)

    def arrive(move):
        move.arrive()

    def arrive_all(group, place):
        if group not in landed:
            landed.add(group)
            pltpu.make_async_copy(place, place, rsem.at[numbers[group]]).wait()

    other_core = {"tile": lo * 2 + 1 - core}
    other_lo = {"tile": (1 - lo) * 2 + core}
    cross = {"tile": (1 - lo) * 2 + 1 - core}

    barrier = pltpu.get_barrier_semaphore()
    peers = [at_y(UP), at_y(DOWN), at_z(UP), at_z(DOWN), other_core, other_lo, cross]
    for peer in peers:
        pl.semaphore_signal(barrier, inc=1, device_id=peer, device_id_type=pl.DeviceIdType.MESH)

    upstream_copy = pltpu.make_async_copy(u_ref, u_vm, lsem.at[1])
    upstream_copy.start()
    own = pltpu.make_async_copy(x_ref, a_buf.at[0, z], lsem.at[2])
    own.start()
    for si in range(3):
        for ri in range(3):
            place = kc.at[:, pl.ds((si * 3 + ri) * width, width)]
            pltpu.make_async_copy(k_ref.at[ri * 3 + si], place, lsem.at[0]).start()
    s_buf[1, :, 2 * taps :] = jnp.zeros((rows, taps), BF16)
    s_buf[cols, :, :taps] = jnp.zeros((rows, taps), BF16)
    with mark("a_barrier"):
        pl.semaphore_wait(barrier, len(peers))

    def part(h):
        return pl.ds(h * half, half)

    def z1(d, h):
        return message(("z1", d, h), x_ref.at[part(h)], a_buf.at[0, z, part(h)], at_z(d))

    def z2(d):
        slot = a_buf.at[0, zed(NEAR[1 - d]), part(d)]
        return message(("z2", d), slot, slot, at_z(d))

    def y1(d, b, h):
        src = x_ref.at[part(h)] if b == 0 else a_buf.at[0, zed(b), part(h)]
        place = a_buf.at[NEAR[1 - d], zed(b), part(h)]
        return message(("y1", d, b, h), src, place, at_y(d), group=None if h == d else ("y1", d))

    def y2(d, b):
        src, place = a_buf.at[NEAR[1 - d], zed(b), part(d)], a_buf.at[2, zed(b), part(d)]
        return message(("y2", d, b), src, place, at_y(d), group=("y2",))

    def columns(p):
        return pl.ds(p * taps, taps)

    def wcore(k, p):
        src = wb.at[2 * k + 1 - core, :, columns(p)]
        return message(("wc", k, p), src, wc_in.at[k, :, columns(p)], other_core, group=("wc", p))

    def wlo(p):
        return message(("wz", p), wz_out.at[:, columns(p)], wz_in.at[:, columns(p)], other_lo)

    def halo_down():
        return message(("halo", 0), u_ref.at[0], halo.at[1], {"tile": tile - 1}, lsem.at[3]).make()

    def halo_up():
        return message(("halo", 1), u_ref.at[rows - 1], halo.at[0], {"tile": tile + 1}, lsem.at[4]).make()

    class Reduce:
        def __init__(self, name, ring, low, count, bufs):
            self.name, self.low, self.count = name, low, count
            self.swap = ring == "z"
            self.first, self.second = (at_z, at_y) if self.swap else (at_y, at_z)
            self.far_in, self.near_in, self.far2_in, self.near2_in = bufs

        def block(self, i, j, h=None):
            low, count = self.low, self.count
            if h is not None:
                count //= 2
                low += h * count
            slot = (j, i) if self.swap else (i, j)
            return (*slot, pl.ds(low, count))

        def far(self, d, k):
            src = p_buf.at[self.block(2, FAR_BLOCKS[d][k])]
            return message((self.name, "far", d, k), src, self.far_in.at[d, k], self.first(d))

        def near(self, d, b):
            src = p_buf.at[self.block(NEAR[d], b)]
            place, group = self.near_in.at[d, b], (self.name, "near", b)
            return message((self.name, "near", d, b), src, place, self.first(d), group=group)

        def far2(self, d):
            src = p_buf.at[self.block(0, 2, d)]
            return message((self.name, "far2", d), src, self.far2_in.at[d], self.second(d))

        def near2(self, d):
            src = p_buf.at[self.block(0, NEAR[d])]
            place, group = self.near2_in.at[d], (self.name, "near2")
            return message((self.name, "near2", d), src, place, self.second(d), group=group)

        def send_far(self, d, k):
            start(self.far(d, k))

        def send_direct(self, b):
            start(self.near(1 - RELAY[b][0], b))

        def send_relayed(self, b):
            d, k = RELAY[b]
            arrive(self.far(d, k))
            slot = self.block(NEAR[d], b)
            p_buf[slot] = (p_buf[slot].astype(F32) + self.far_in[d, k].astype(F32)).astype(BF16)
            start(self.near(d, b))

        def near_sum(self, b):
            arrive_all((self.name, "near", b), self.near_in.at[:, b])
            own_term = p_buf[self.block(0, b)].astype(F32)
            return own_term + self.near_in[UP, b].astype(F32) + self.near_in[DOWN, b].astype(F32)

        def send_far2(self):
            p_buf[self.block(0, 2)] = self.near_sum(2).astype(BF16)
            for d in BOTH:
                start(self.far2(d))

        def send_near2(self, d):
            b, n = NEAR[d], self.count // 2
            total = self.near_sum(b)
            arrive(self.far2(d))
            p_buf[self.block(0, b, 1 - d)] = total[(1 - d) * n : (2 - d) * n].astype(BF16)
            p_buf[self.block(0, b, d)] = (
                total[d * n : (d + 1) * n] + self.far2_in[d].astype(F32)
            ).astype(BF16)
            start(self.near2(d))

        def finish(self):
            total = self.near_sum(0)
            arrive_all((self.name, "near2"), self.near2_in)
            total += self.near2_in[UP].astype(F32) + self.near2_in[DOWN].astype(F32)
            place = pl.ds(self.low, self.count)
            gi_ref[place] = jnp.where(a_buf[0, z, place] > 0, total, 0.0).astype(BF16)

    first, last = tile == 0, tile == 3

    @pl.when(jnp.logical_not(first))
    def _():
        halo_down().start()

    @pl.when(jnp.logical_not(last))
    def _():
        halo_up().start()

    for h in BOTH:
        for d in BOTH:
            start(z1(d, h ^ d))
        for d in BOTH:
            start(y1(d, 0, h ^ d))

    with mark("b_uf"):
        upstream_copy.wait()

        @pl.loop(0, rows)
        def _(i):
            uf[pl.ds(pl.multiple_of((i + 1) * cols, 8), cols), :] = u_vm[i].astype(F32)

    bottom = (rows + 1) * cols
    with mark("c_halo"):

        @pl.when(first)
        def _():
            uf[:cols, :] = jnp.zeros((cols, width), F32)

        @pl.when(jnp.logical_not(first))
        def _():
            halo_up().wait_recv()
            uf[:cols, :] = halo[0].astype(F32)

        @pl.when(last)
        def _():
            uf[bottom:, :] = jnp.zeros((cols, width), F32)

        @pl.when(jnp.logical_not(last))
        def _():
            halo_down().wait_recv()
            uf[bottom:, :] = halo[1].astype(F32)

    with mark("d_im2col"):

        @pl.loop(0, cols)
        def _(j):
            for ri in range(3):
                value = uf[pl.ds((2 - ri) * cols + j, rows, stride=cols), :].astype(BF16)
                for si in range(3):
                    s_buf[j + si, :, pl.ds(si * taps + ri * width, width)] = value

        pltpu.make_async_copy(kc, kc, lsem.at[0]).wait()

    def stacked(a, lanes=slice(None)):
        block = s_buf[pl.ds(ycoord(a) * group_cols + 1, group_cols), :, lanes]
        return block.reshape(NZ * chunk, block.shape[2])

    def dgrad(a):
        value = lax.dot_general(
            stacked(a), kc[...], (((1,), (1,)), ((), ())), preferred_element_type=F32
        ).astype(BF16)
        for place in range(NZ):
            p_buf[a, lax.rem(place - z + NZ, NZ)] = value[place * chunk : (place + 1) * chunk]

    def activate(a):
        chunks = a_buf[a].reshape(NZ * chunk, a_buf.shape[3])
        at[...] = jnp.maximum(chunks, jnp.zeros((), BF16)).T

    def wgrad(a):
        activate(a)
        value = jnp.dot(at[...], stacked(a), preferred_element_type=F32).reshape(wacc.shape)
        if a == 0:
            wacc[...] = value
        else:
            wacc[...] += value

    def wgrad_z():
        own.wait()
        for d in BOTH:
            for h in BOTH:
                arrive(z1(d, h))
            arrive(z2(d))
        wgrad(0)

    def wgrad_y(d):
        for b in range(NZ):
            arrive(y1(d, b, d))
        arrive_all(("y1", d), a_buf.at[NEAR[1 - d], :, part(1 - d)])
        wgrad(NEAR[1 - d])

    def wgrad_last(p):
        if p == 0:
            arrive_all(("y2",), a_buf.at[2])
            activate(2)
        value = jnp.dot(at[...], stacked(2, columns(p)), preferred_element_type=F32)
        wacc[:, :, columns(p)] += value.reshape(wacc.shape[0], wacc.shape[1], taps)

    def wcore_out(p):
        wb[:, :, columns(p)] = wacc[:, :, columns(p)].astype(BF16)
        for k in (0, 1):
            start(wcore(k, p))

    def wlo_out(p):
        arrive_all(("wc", p), wc_in.at[:, :, columns(p)])
        total = wacc[2 * (1 - lo) + core, :, columns(p)] + wc_in[1 - lo, :, columns(p)].astype(F32)
        wz_out[:, columns(p)] = total.astype(BF16)
        start(wlo(p))

    def wgrad_out(p):
        arrive(wlo(p))
        grad = wacc[tile, :, columns(p)] + wc_in[lo, :, columns(p)].astype(F32)
        grad += wz_in[:, columns(p)].astype(F32)
        for ri in range(3):
            gk_ref[ri * 3 + p] = grad[:, ri * width : (ri + 1) * width]

    def pass_z(d):
        arrive(z1(d, d))
        start(z2(d))

    def pass_to_y(e, b, h):
        arrive(z2(h) if b == 2 else z1(UP if b == 3 else DOWN, h))
        start(y1(e, b, h))

    def pass_y(d, b):
        arrive(y1(d, b, d))
        start(y2(d, b))

    steps = {
        "wgrad0": wgrad_z,
        "wgrad3": functools.partial(wgrad_y, UP),
        "wgrad1": functools.partial(wgrad_y, DOWN),
    }
    for a in range(NY):
        steps[f"dgrad{a}"] = functools.partial(dgrad, a)
    for d in BOTH:
        steps[f"z2_{d}"] = functools.partial(pass_z, d)
        for b in range(NZ):
            steps[f"pass{d}{b}"] = functools.partial(pass_y, d, b)
        for b in (1, 2, 3):
            for h in BOTH:
                steps[f"y1_{d}{b}{h}"] = functools.partial(pass_to_y, d, b, h)
    for p in range(W_PARTS):
        steps[f"wgrad2_{p}"] = functools.partial(wgrad_last, p)
        steps[f"wcore_{p}"] = functools.partial(wcore_out, p)
        steps[f"wlo_{p}"] = functools.partial(wlo_out, p)
        steps[f"wfin_{p}"] = functools.partial(wgrad_out, p)
    low = 0
    for n, (name, ring, count) in enumerate(CLASSES):
        red = Reduce(name, ring, low, count, landing[4 * n : 4 * n + 4])
        low += count
        for d in BOTH:
            for k in (0, 1):
                steps[f"{name}_far{k}{d}"] = functools.partial(red.send_far, d, k)
            steps[f"{name}_near2{d}"] = functools.partial(red.send_near2, d)
        for b in range(NZ):
            steps[f"{name}_dir{b}"] = functools.partial(red.send_direct, b)
            steps[f"{name}_dep{b}"] = functools.partial(red.send_relayed, b)
        steps[f"{name}_far2"] = red.send_far2
        steps[f"{name}_fin"] = red.finish
    listed = list(steps.items())
    assert sorted(ORDER) == list(range(len(listed)))
    for n, place in enumerate(ORDER):
        name, step = listed[place]
        with mark(f"{n:03}_{name}"):
            step()
    assert len(numbers) == MESSAGES
    with mark("y_sends"):
        column = rows * 9 * width * 2
        assert sum(sent) % column == 0
        everything = s_buf.at[pl.ds(0, sum(sent) // column)]
        pltpu.make_async_copy(everything, everything, ssem.at[0]).wait()

        @pl.when(jnp.logical_not(first))
        def _():
            halo_down().wait_send()

        @pl.when(jnp.logical_not(last))
        def _():
            halo_up().wait_send()


def write_out(gi_ref, gk_ref, gi_out, gk_out, sem):
    copies = [
        pltpu.make_async_copy(gi_ref, gi_out, sem.at[0]),
        pltpu.make_async_copy(gk_ref, gk_out, sem.at[1]),
    ]
    for copy in copies:
        copy.start()
    for copy in copies:
        copy.wait()


def per_device(saved_input, upstream, weights):
    rows, cols, width = upstream.shape
    own_cols, channels = saved_input.shape[1], saved_input.shape[2]
    chunk = own_cols * rows
    x = jnp.transpose(saved_input, (1, 0, 2)).reshape(chunk, channels)
    hbm = pl.BlockSpec(memory_space=pl.ANY)
    vmem = pl.BlockSpec(memory_space=pltpu.VMEM)
    block = channels // 4
    gi_shape, gk_shape = (chunk, channels), (9, block, width)
    landing = []
    for _, _, n in CLASSES:
        for shape in ((2, 2, n), (2, NZ, n), (2, n // 2), (2, n)):
            landing.append(pltpu.VMEM((*shape, channels), BF16))
    gi, gk = pl.pallas_call(
        kernel,
        name="conv_backward",
        out_shape=(pltpu.VMEM(gi_shape, BF16), pltpu.VMEM(gk_shape, F32)),
        in_specs=[hbm, hbm, hbm],
        out_specs=(vmem, vmem),
        scratch_shapes=[
            pltpu.VMEM((rows, cols, width), BF16),
            pltpu.VMEM((channels, 9 * width), BF16),
            pltpu.VMEM(((rows + 2) * cols, width), F32),
            pltpu.VMEM((cols + 2, rows, 9 * width), BF16),
            pltpu.VMEM((NY, NZ, chunk, channels), BF16),
            pltpu.VMEM((NY, NZ, chunk, channels), BF16),
            pltpu.VMEM((4, block, 9 * width), F32),
            pltpu.VMEM((channels, NZ * chunk), BF16),
            pltpu.VMEM((4, block, 9 * width), BF16),
            pltpu.VMEM((2, block, 9 * width), BF16),
            pltpu.VMEM((block, 9 * width), BF16),
            pltpu.VMEM((block, 9 * width), BF16),
            pltpu.VMEM((2, cols, width), BF16),
            pltpu.SemaphoreType.DMA((1,)),
            pltpu.SemaphoreType.DMA((MESSAGES,)),
            pltpu.SemaphoreType.DMA((5,)),
            *landing,
        ],
        compiler_params=pltpu.CompilerParams(
            collective_id=0, has_side_effects=True, vmem_limit_bytes=56 * 1024 * 1024
        ),
    )(x, upstream, weights.reshape(9, channels, width))
    gi, gk = pl.pallas_call(
        write_out,
        name="write_out",
        out_shape=(jax.ShapeDtypeStruct(gi_shape, BF16), jax.ShapeDtypeStruct(gk_shape, F32)),
        in_specs=[vmem, vmem],
        out_specs=(hbm, hbm),
        scratch_shapes=[pltpu.SemaphoreType.DMA((2,))],
        compiler_params=pltpu.CompilerParams(vmem_limit_bytes=1024 * 1024),
    )(gi, gk)
    input_grad = jnp.transpose(gi.reshape(own_cols, rows, channels), (1, 0, 2))
    return input_grad, gk.reshape(3, 3, block, width)


def solution(mesh):
    placed = (P("tile", "filt", "chan"), P("tile", None, "filt"), P(None, None, "chan", "filt"))
    return jax.shard_map(
        per_device,
        mesh=mesh,
        in_specs=placed,
        out_specs=(P("tile", "filt", "chan"), P(None, None, ("chan", "tile"), "filt")),
        check_vma=False,
    )
```
